128 devices in a mesh: doc: 8 (over x_lo, z), term: 16 (over y, x_hi, core).
Axes of the slice: x: 4 (x_hi: 2, x_lo: 2; x = x_hi * 2 + x_lo), y: 4, z: 4, core: 2. Of those that a mesh axis runs over, the one named last changes fastest.
Arguments:
- tiles: bfloat16 [8, 16, 8, 512, 512], P('doc', 'term'), may hold values from 0.0009994507 to 1
- tile_rows: int32 [8, 16, 8], P('doc', 'term'), may hold values from 0 to 31, as said below
- tile_cols: int32 [8, 16, 8], P('doc', 'term'), may hold values from 0 to 63
- counts: int32 [8, 16], P('doc', 'term'), may hold values from 2 to 8, as said below
- start_block: float32 [16, 524288], P(None, 'term'), may hold values from -6 to 6
Outputs:
- left_block: float32 [16, 131072], P(None, ('doc', 'term'))
- right_block: float32 [16, 524288], P(None, ('term', 'doc'))
- coefficients: float32 [5, 16, 16], replicated
The draws below stay inside these ranges and needn't reach their ends.
Inputs may be any that keep to these rules, and one draw needn't show every extreme that they name: On each device the pairs (tile_rows, tile_cols) of its 8 slots are distinct. `counts`: some device uses all 8 slots.
All inputs are finite; a program needn't handle non-finite values.
Results may differ from the reference program's by a relative error of at most 0.0031.
Values sent between devices are 32-bit elements; how exact they have to be, the bound alone decides.
A program may use at most 64 MiB of HBM per device.

```python
import math
import jax
import jax.numpy as jnp
from jax import lax

TILE = 512
BLOCK = 16
TERM_TILES = 64
DOC_TILES = 32
SLOTS = 8
NTERM = 524288
N_DOC = 8
N_TERM = 16


def pick_slots(subkey):
    return jax.random.permutation(subkey, DOC_TILES * TERM_TILES)[:SLOTS]


def tile_positions(key):
    subkeys = jax.random.split(jax.random.fold_in(key, 11), N_DOC * N_TERM)
    picked = jax.vmap(pick_slots)(subkeys)
    return picked.reshape(N_DOC, N_TERM, SLOTS).astype(jnp.int32)


def draw_tile_rows(key, part):
    return (tile_positions(key) // TERM_TILES).astype(jnp.int32)


def draw_tile_cols(key, part):
    return (tile_positions(key) % TERM_TILES).astype(jnp.int32)


def draw_counts(key, part):
    devices = N_DOC * N_TERM
    base = jax.random.randint(jax.random.fold_in(key, 5), (devices,), SLOTS // 4, SLOTS + 1)
    chosen = jax.random.randint(jax.random.fold_in(key, 6), (), 0, devices)
    filled = jnp.where(jnp.arange(devices) == chosen, SLOTS, base)
    return filled.reshape(N_DOC, N_TERM).astype(jnp.int32)


def shard_levels(key, shape, shards, least, top_value):
    def one(dim, shards_of):
        draws = jax.random.uniform(jax.random.fold_in(jax.random.fold_in(key, 6), dim), (shards_of,), jnp.float32, least / len(shards), top_value / len(shards))
        return jnp.repeat(jnp.exp(draws), shape[dim] // shards_of).reshape((-1,) + (1,) * (len(shape) - dim - 1))

    loudness = one(*shards[0])
    for cut in shards[1:]:
        loudness = loudness * one(*cut)
    return loudness


def bell_draw(rng, shape, deviation, most, shards=(), held_as=jnp.bfloat16):
    array = deviation * jax.random.normal(rng, shape, jnp.float32)
    if shards:
        array = array * shard_levels(rng, shape, shards, -0.22, 0.18)
    return jnp.clip(array, -most, most).astype(held_as)


def setup_inputs(seed: int = 0) -> dict:
    splits = jax.random.split(jax.random.key(seed), 6)
    return {
        "tiles": jnp.clip(jnp.exp(math.log(1.0) - 6.9083047 * jax.random.uniform(splits[0], (N_DOC, N_TERM, SLOTS, TILE, TILE), jnp.float32) ** shard_levels(splits[0], (N_DOC, N_TERM, SLOTS, TILE, TILE), ((0, 8), (1, 16)), -0.2, 0.2)), 0.0009994507, 1.0).astype(jnp.bfloat16),
        "tile_rows": draw_tile_rows(jax.random.fold_in(splits[5], 71), 0),
        "tile_cols": draw_tile_cols(jax.random.fold_in(splits[5], 71), 0),
        "counts": draw_counts(jax.random.fold_in(splits[5], 71), 0),
        "start_block": bell_draw(splits[4], (BLOCK, NTERM), 1.0, 6.0, ((1, 16),), jnp.float32),
    }


def orthonormal(vectors, total_rows):
    highest = lax.Precision.HIGHEST
    gram_matrix = jnp.dot(vectors, vectors.T, precision=highest) / total_rows
    factor = jnp.linalg.cholesky(gram_matrix)
    return (jax.scipy.linalg.solve_triangular(factor, vectors, lower=True), factor)

def projected(vectors, earlier, total_rows):
    highest = lax.Precision.HIGHEST
    projection = jnp.dot(vectors, earlier.T, precision=highest) / total_rows
    return (vectors - jnp.dot(projection, earlier, precision=highest), projection)

def reference(tiles, tile_rows, tile_cols, counts, start_block):
    highest = lax.Precision.HIGHEST
    n_docs = N_DOC * DOC_TILES * TILE
    n_terms = N_TERM * TERM_TILES * TILE
    devices = N_DOC * N_TERM
    active = (jnp.arange(SLOTS)[None, None, :] < counts[:, :, None]).astype(jnp.float32)
    row_onehot = (tile_rows[..., None] == jnp.arange(DOC_TILES)[None, None, None, :]).astype(jnp.float32)
    col_onehot = (tile_cols[..., None] == jnp.arange(TERM_TILES)[None, None, None, :]).astype(jnp.float32)
    row_live = row_onehot * active[..., None]
    col_live = col_onehot * active[..., None]

    def device_degrees(index):
        doc_index = index // N_TERM
        term_index = index % N_TERM
        values = tiles[doc_index, term_index].astype(jnp.float32)
        row_sums = lax.optimization_barrier(jnp.sum(values, axis=2))
        col_sums = lax.optimization_barrier(jnp.sum(values, axis=1))
        row_part = jnp.einsum('kr,ka->ra', row_live[doc_index, term_index], row_sums, precision=highest)
        col_part = jnp.einsum('kc,kb->cb', col_live[doc_index, term_index], col_sums, precision=highest)
        return (row_part.reshape(-1), col_part.reshape(-1))
    row_parts, col_parts = lax.map(device_degrees, jnp.arange(devices))
    row_degree = 1.0 + lax.optimization_barrier(jnp.sum(row_parts.reshape(N_DOC, N_TERM, -1), axis=1)).reshape(-1)
    col_degree = 1.0 + lax.optimization_barrier(jnp.sum(col_parts.reshape(N_DOC, N_TERM, -1), axis=0)).reshape(-1)
    row_scale = lax.rsqrt(row_degree)
    col_scale = lax.rsqrt(col_degree)

    def forward(right_block):
        scaled = (right_block * col_scale[None, :]).astype(jnp.bfloat16).astype(jnp.float32)
        scaled = scaled.reshape(BLOCK, N_TERM, TERM_TILES, TILE)

        def device_forward(index):
            doc_index = index // N_TERM
            term_index = index % N_TERM
            local_right = scaled[:, term_index]
            pieces = jnp.einsum('kc,bcx->kbx', col_onehot[doc_index, term_index], local_right, precision=highest)
            values = tiles[doc_index, term_index].astype(jnp.float32)
            product = jnp.einsum('kab,kcb->kca', values, pieces, precision=highest)
            return jnp.einsum('kr,kca->cra', row_live[doc_index, term_index], product, precision=highest).reshape(BLOCK, -1)
        parts = lax.map(device_forward, jnp.arange(devices))
        summed = lax.optimization_barrier(jnp.sum(parts.reshape(N_DOC, N_TERM, BLOCK, -1), axis=1))
        return summed.transpose(1, 0, 2).reshape(BLOCK, -1) * row_scale[None, :]

    def backward(left_block):
        scaled = (left_block * row_scale[None, :]).astype(jnp.bfloat16).astype(jnp.float32)
        scaled = scaled.reshape(BLOCK, N_DOC, DOC_TILES, TILE)

        def device_backward(index):
            doc_index = index // N_TERM
            term_index = index % N_TERM
            local_left = scaled[:, doc_index]
            pieces = jnp.einsum('kr,brx->kbx', row_onehot[doc_index, term_index], local_left, precision=highest)
            values = tiles[doc_index, term_index].astype(jnp.float32)
            product = jnp.einsum('kab,kca->kcb', values, pieces, precision=highest)
            return jnp.einsum('kc,kxb->xcb', col_live[doc_index, term_index], product, precision=highest).reshape(BLOCK, -1)
        parts = lax.map(device_backward, jnp.arange(devices))
        summed = lax.optimization_barrier(jnp.sum(parts.reshape(N_DOC, N_TERM, BLOCK, -1), axis=0))
        return summed.transpose(1, 0, 2).reshape(BLOCK, -1) * col_scale[None, :]
    first_right, factor_zero = orthonormal(start_block, n_terms)
    left_one, factor_one = orthonormal(forward(first_right), n_docs)
    right_raw, projection_one = projected(backward(left_one), first_right, n_terms)
    right_two, factor_two = orthonormal(right_raw, n_terms)
    left_raw, projection_two = projected(forward(right_two), left_one, n_docs)
    left_two, factor_three = orthonormal(left_raw, n_docs)
    coefficients = jnp.stack([factor_one, projection_one, factor_two, projection_two, factor_three])
    return (left_two, right_two, coefficients)
```

```python
import functools

import jax
import jax.numpy as jnp
from jax import lax
from jax.experimental import pallas as pl
from jax.experimental.pallas import tpu as pltpu
from jax.sharding import PartitionSpec as P

MESH = pl.DeviceIdType.MESH
F32 = jnp.float32
BF16 = jnp.bfloat16
TILE = 512
BLOCK = 16
SLOTS = 8
LANES = SLOTS * BLOCK
TERM_TILES = 64
DOC_TILES = 32
ND = 8
NT = 16
DX = TILE // ND
TX = TILE // NT
DGROUPS = DOC_TILES * BLOCK // LANES
TGROUPS = TERM_TILES * BLOCK // LANES
N_DOCS = ND * DOC_TILES * TILE
N_TERMS = NT * TERM_TILES * TILE
HIGHEST = lax.Precision.HIGHEST


def dot(a, b, contract, precision=HIGHEST):
    return lax.dot_general(
        a, b, (contract, ((), ())), precision=precision, preferred_element_type=F32
    )


NN = ((1,), (0,))
NTR = ((1,), (1,))
TN = ((0,), (0,))


def halves(x):
    hi = x.astype(BF16)
    lo = (x - hi.astype(F32)).astype(BF16)
    return jnp.concatenate([hi, lo], axis=0)


def by_onehot(x, onehot, contract):
    n = x.shape[0]
    both = dot(halves(x), onehot, contract, None)
    return both[:n] + both[n:]


def iota(shape, dim):
    return lax.broadcasted_iota(jnp.int32, shape, dim)


def roll(x, shift):
    return pltpu.roll(x, shift, 1)


def fold(t):
    same = iota((LANES, LANES), 0) // BLOCK == iota((LANES, LANES), 1) // BLOCK
    t = jnp.where(same, t, 0.0)
    w = t[0:BLOCK]
    for g in range(1, SLOTS):
        w = w + t[g * BLOCK : (g + 1) * BLOCK]
    w = w + roll(w, 64)
    w = w + roll(w, 32)
    return w + roll(w, 16)


def packed(s, r):
    group = iota((8, LANES), 1) // BLOCK
    z = jnp.where(group == 0, s[0:8], s[8:16])
    if r is None:
        return z
    return jnp.where(group < 2, z, jnp.where(group == 2, r[0:8], r[8:16]))


def unpacked(z, first):
    lane = iota((BLOCK, LANES), 1)
    top = z if first == 0 else roll(z, LANES - BLOCK * first)
    low = roll(z, LANES - BLOCK * (first + 1))
    return jnp.where(lane < BLOCK, jnp.concatenate([top, low], axis=0), 0.0)


def spread(m):
    same = iota((LANES, LANES), 0) // BLOCK == iota((LANES, LANES), 1) // BLOCK
    r = m + roll(m, 16)
    r = r + roll(r, 32)
    r = r + roll(r, 64)
    return jnp.where(same, jnp.concatenate([r] * SLOTS, axis=0), 0.0)


def factor(s):
    lane = iota((BLOCK, LANES), 1)
    sub = iota((BLOCK, LANES), 0)
    m = jnp.where(lane < BLOCK, s, jnp.where(lane == sub + BLOCK, 1.0, 0.0))
    for c in range(BLOCK - 1):
        ratio = m[c : c + 1, :] / m[c : c + 1, c : c + 1]
        m = m - jnp.where(sub > c, m[:, c : c + 1], 0.0) * ratio
    diag = jnp.sum(jnp.where(lane == sub, m, 0.0), axis=1, keepdims=True)
    m = m * lax.rsqrt(diag)
    upper = jnp.where((lane < BLOCK) & (lane >= sub), m, 0.0)
    inverse = jnp.where(lane < BLOCK, roll(m, LANES - BLOCK), 0.0)
    return upper, inverse


def transposed(m):
    full = jnp.concatenate([m, jnp.zeros((LANES - BLOCK, LANES), F32)], axis=0)
    return full.T[:BLOCK, :]


def kernel(
    rows_s, cols_s, cnt_s, tiles_h, start_h,
    left_o, right_o, coef_o,
    tiles_v, start_v, st_v, sd_v,
    m1_v, d1_v, cs_v,
    tsend, trecv, dsend, drecv, za, zb,
    slots_v, share_v, e_v, u_v, x_v,
    load_sem, send_sem, recv_sem,
):
    i = lax.axis_index("doc")
    j = lax.axis_index("term")
    bar = pltpu.get_barrier_semaphore()
    for d in range(1, ND):
        pl.semaphore_signal(bar, 1, device_id=(lax.rem(i + d, ND), j), device_id_type=MESH)
    for d in range(1, NT):
        pl.semaphore_signal(bar, 1, device_id=(i, lax.rem(j + d, NT)), device_id_type=MESH)

    def load_start(t, carry):
        columns = pl.ds(pl.multiple_of(t * TILE, TILE), TILE)
        pltpu.make_async_copy(start_h.at[:, columns], start_v.at[t], load_sem.at[SLOTS]).start()
        return carry

    lax.fori_loop(0, TERM_TILES, load_start, 0)
    loads = []
    for k in range(SLOTS):
        load = pltpu.make_async_copy(tiles_h.at[k], tiles_v.at[k], load_sem.at[k])
        load.start()
        loads.append(load)

    pending = []

    def to_terms(n, src_of, dst, size):
        def send(d, carry):
            q = lax.rem(j + d, NT)
            pltpu.make_async_remote_copy(
                src_ref=src_of(q), dst_ref=dst.at[j],
                send_sem=send_sem.at[n], recv_sem=recv_sem.at[n],
                device_id=(i, q), device_id_type=MESH,
            ).start()
            return carry
        lax.fori_loop(1, NT, send, 0)
        pending.append((n, dst.at[pl.ds(0, NT - 1)]))

    def to_docs(n, src_of, dst, size):
        def send(d, carry):
            q = lax.rem(i + d, ND)
            pltpu.make_async_remote_copy(
                src_ref=src_of(q), dst_ref=dst.at[i],
                send_sem=send_sem.at[n], recv_sem=recv_sem.at[n],
                device_id=(q, j), device_id_type=MESH,
            ).start()
            return carry
        lax.fori_loop(1, ND, send, 0)
        pending.append((n, dst.at[pl.ds(0, ND - 1)]))

    def arrived(n, dst, peers):
        part = dst.at[pl.ds(0, peers - 1)]
        pltpu.make_async_copy(part, part, recv_sem.at[n]).wait()

    lane8 = iota((8, LANES), 1)
    sub8 = iota((8, LANES), 0)
    cnt = cnt_s[0]
    row_at = jnp.zeros((8, LANES), jnp.int32)
    my_col = jnp.zeros((8, LANES), jnp.int32)
    col_of = jnp.zeros((8, LANES), jnp.int32)
    for k in range(SLOTS):
        here = lane8 // BLOCK == k
        row_at = jnp.where(here, rows_s[k] * BLOCK, row_at)
        my_col = jnp.where(here, cols_s[k], my_col)
        col_of = jnp.where(sub8 == k, cols_s[k], col_of)
    row_at = jnp.where(lane8 // BLOCK < cnt, row_at, -100000)
    my_col = jnp.where(lane8 // BLOCK < cnt, my_col, -10000)
    col_of = jnp.where(sub8 < cnt, col_of, -10000)
    col_at = my_col * BLOCK
    row_at = (row_at + lane8 % BLOCK).astype(F32)
    col_at = (col_at + lane8 % BLOCK).astype(F32)
    my_col = my_col.astype(F32)
    d1_v[i] = jnp.concatenate([col_of.astype(F32), col_at], axis=0)

    pltpu.make_async_copy(start_v, start_v, load_sem.at[SLOTS]).wait()
    acc = jnp.zeros((2 * LANES, 2 * LANES), F32)
    for ch in range(8):
        both = halves(start_v[ch * 8 : (ch + 1) * 8].reshape(LANES, TILE))
        acc = acc + dot(both, both, NTR, None)
    t = acc[:LANES, :LANES] + acc[:LANES, LANES:] + acc[LANES:, :LANES] + acc[LANES:, LANES:]
    m1_v[j] = jnp.concatenate([packed(fold(t) * (1.0 / N_TERMS), None), row_at], axis=0)

    col_sums = jnp.zeros((16, TILE), F32)
    for k in range(SLOTS):
        loads[k].wait()
        ones = jnp.where(iota((16, TILE), 0) == k, 1.0, 0.0).astype(BF16)
        col_sums = col_sums + dot(ones, tiles_v[k], NN, None)
    cs_v[i] = col_sums[:SLOTS]

    pl.semaphore_wait(bar, ND - 1 + NT - 1)
    to_docs(0, lambda q: d1_v.at[i], d1_v, 0)
    to_docs(1, lambda q: cs_v.at[i], cs_v, 0)
    to_terms(2, lambda q: m1_v.at[j], m1_v, 0)

    lane_slot = iota((TILE, LANES), 1) // BLOCK

    def forward_product(x, out):
        total = None
        for k in range(SLOTS):
            part = dot(tiles_v[k], jnp.where(lane_slot == k, x, 0.0).astype(BF16), NN, None)
            total = part if total is None else total + part
        for q in range(NT):
            out[q] = total[q * TX : (q + 1) * TX]

    forward_product(jnp.ones((TILE, LANES), F32), tsend.at[0])
    trecv[0, j] = tsend[0, j]
    to_terms(3, lambda q: tsend.at[0, q], trecv.at[0], 0)

    slots_v[...] = jnp.concatenate([start_v[cols_s[k]] for k in range(SLOTS)], axis=0).T
    window = pl.ds(pl.multiple_of(128 * (i // 2), 128), 128)
    for g in range(TGROUPS):
        share_v[g] = start_v[g * 8 : (g + 1) * 8, :, window].reshape(LANES, 128).T
    half = pl.multiple_of(DX * lax.rem(i, 2), DX)
    start_share = jnp.concatenate([share_v[g, pl.ds(half, DX), :] for g in range(TGROUPS)], axis=0)
    e_v[...] = start_share

    arrived(0, d1_v, ND)
    arrived(1, cs_v, ND)
    cols_in = jnp.concatenate([d1_v[q, 0:8, :] for q in range(ND)], axis=0)
    sums_t = jnp.concatenate([cs_v[q] for q in range(ND)], axis=0).T
    same_col = jnp.where(cols_in == my_col[0:1, :], 1.0, 0.0)
    col_scale = lax.rsqrt(dot(sums_t, same_col, NN) + 1.0)
    arrived(2, m1_v, NT)
    gram = m1_v[0, 0:8, :]
    for q in range(1, NT):
        gram = gram + m1_v[q, 0:8, :]
    _, inverse0 = factor(unpacked(gram, 0))
    k0 = spread(inverse0)
    scaled_e = dot(slots_v[...], k0, NTR) * col_scale
    slots_v[...] = scaled_e
    forward_product(scaled_e, tsend.at[1])
    trecv[1, j] = tsend[1, j]
    to_terms(4, lambda q: tsend.at[1, q], trecv.at[1], 0)

    for q in range(NT):
        hit = iota((DOC_TILES * BLOCK, LANES), 0).astype(F32) == m1_v[q, 8:9, :]
        st_v[:, q * LANES : (q + 1) * LANES] = jnp.where(hit, 1.0, 0.0).astype(BF16)
    arrived(3, trecv.at[0], NT)

    def term_sum(n):
        flat = jnp.concatenate([trecv[n, q] for q in range(NT)], axis=1)
        return by_onehot(flat, st_v[...], NTR)

    def stacked(x, groups):
        return jnp.concatenate([x[:, g * LANES : (g + 1) * LANES] for g in range(groups)], axis=0)

    def flat_of(x, groups):
        n = x.shape[0] // groups
        return jnp.concatenate([x[g * n : (g + 1) * n] for g in range(groups)], axis=1)

    row_scale = stacked(lax.rsqrt(term_sum(0) + 1.0), DGROUPS)
    e_share = dot(e_v[...], k0, NTR)
    e_v[...] = e_share
    for q in range(ND):
        hit = iota((TERM_TILES * BLOCK, LANES), 0).astype(F32) == d1_v[q, 8:9, :]
        sd_v[:, q * LANES : (q + 1) * LANES] = jnp.where(hit, 1.0, 0.0).astype(BF16)
    cols_wide = jnp.concatenate([cols_in] * TGROUPS, axis=1)
    tile_at = (iota((ND * SLOTS, TERM_TILES * BLOCK), 1) // BLOCK).astype(F32)
    x_v[0:TILE, 0 : ND * SLOTS] = sums_t
    my_sums = x_v[pl.ds(pl.multiple_of(i * DX, DX), DX), 0 : ND * SLOTS]
    col_share = stacked(
        lax.rsqrt(dot(my_sums, jnp.where(cols_wide == tile_at, 1.0, 0.0), NN) + 1.0), TGROUPS
    )

    def all_sum(n, base, z):
        za[n, i] = z
        to_docs(base, lambda q: za.at[n, i], za.at[n], 0)

        def rest():
            arrived(base, za.at[n], ND)
            s = za[n, 0]
            for q in range(1, ND):
                s = s + za[n, q]
            zb[n, j] = s
            to_terms(base + 1, lambda q: zb.at[n, j], zb.at[n], 0)

        def last():
            arrived(base + 1, zb.at[n], NT)
            s = zb[n, 0]
            for q in range(1, NT):
                s = s + zb[n, q]
            return s

        return rest, last

    def term_gather(n, x):
        wide = by_onehot(flat_of(x, DGROUPS), st_v[...], NN)
        for q in range(NT):
            tsend[n, q] = wide[:, q * LANES : (q + 1) * LANES]

    arrived(4, trecv.at[1], NT)
    f1 = stacked(term_sum(1), DGROUPS) * row_scale
    rest, last = all_sum(0, 5, packed(fold(dot(f1, f1, TN)) * (1.0 / N_DOCS), None))
    term_gather(2, f1 * row_scale)
    trecv[2, j] = tsend[2, j]
    rest()
    to_terms(7, lambda q: tsend.at[2, q], trecv.at[2], 0)
    upper1, inverse1 = factor(unpacked(last(), 0))
    k1 = spread(inverse1)
    arrived(7, trecv.at[2], NT)
    pieces = jnp.concatenate([trecv[2, q] for q in range(NT)], axis=0)
    yt = dot(k1, pieces, NTR).astype(BF16)
    back = jnp.concatenate(
        [dot(yt[k * BLOCK : (k + 1) * BLOCK], tiles_v[k], NN, None) for k in range(SLOTS)], axis=0
    ).T
    for q in range(ND):
        dsend[0, q] = back[q * DX : (q + 1) * DX]
    drecv[0, i] = dsend[0, i]
    to_docs(8, lambda q: dsend.at[0, q], drecv.at[0], 0)

    u1 = dot(f1, k1, NTR)
    for g in range(DGROUPS):
        u_v[g] = u1[g * TX : (g + 1) * TX]
    p0 = upper1 * (N_DOCS / N_TERMS)
    expected = dot(e_share, spread(p0), NTR)

    arrived(8, drecv.at[0], ND)
    flat = jnp.concatenate([drecv[0, q] for q in range(ND)], axis=1)
    b1 = stacked(by_onehot(flat, sd_v[...], NTR), TGROUPS) * col_share - expected
    t2 = dot(b1, jnp.concatenate([b1, e_v[...]], axis=1), TN) * (1.0 / N_TERMS)
    rest, last = all_sum(1, 9, packed(fold(t2[:, :LANES]), fold(t2[:, LANES:])))
    for g in range(TGROUPS):
        share_v[g, 0:DX, :] = b1[g * DX : (g + 1) * DX]
    wide = by_onehot(flat_of(b1 * col_share, TGROUPS), sd_v[...], NN)
    for q in range(ND):
        dsend[1, q] = wide[:, q * LANES : (q + 1) * LANES]
    drecv[1, i] = dsend[1, i]
    to_docs(11, lambda q: dsend.at[1, q], drecv.at[1], 0)
    rest()
    z = last()
    r1 = unpacked(z, 2)
    pad = jnp.zeros((LANES - BLOCK, LANES), F32)
    g2 = unpacked(z, 0) - dot(r1, jnp.concatenate([r1, pad], axis=0), NTR)
    upper2, inverse2 = factor(g2)
    k2 = spread(inverse2)
    kr1 = spread(r1)
    arrived(11, drecv.at[1], ND)
    pieces = jnp.concatenate([drecv[1, q] for q in range(ND)], axis=0)
    pieces = pieces - dot(slots_v[...], kr1, NTR)
    forward_product(dot(pieces, k2, NTR), tsend.at[3])
    trecv[3, j] = tsend[3, j]
    to_terms(12, lambda q: tsend.at[3, q], trecv.at[3], 0)

    drecv[2, i] = share_v[i, 0:DX, :]
    to_docs(13, lambda q: share_v.at[q, pl.ds(0, DX), :], drecv.at[2], 0)
    trecv[4, j] = u_v[j // 4]
    to_terms(14, lambda q: u_v.at[q // 4], trecv.at[4], 0)
    p02 = upper2 * (N_TERMS / N_DOCS)
    expected = dot(u1, spread(p02), NTR)

    arrived(12, trecv.at[3], NT)
    f2 = stacked(term_sum(3), DGROUPS) * row_scale - expected
    t3 = dot(f2, jnp.concatenate([f2, u1], axis=1), TN) * (1.0 / N_DOCS)
    rest, last = all_sum(2, 15, packed(fold(t3[:, :LANES]), fold(t3[:, LANES:])))
    for g in range(DGROUPS):
        x_v[g * TX : (g + 1) * TX, :] = f2[g * TX : (g + 1) * TX]
    trecv[5, j] = x_v[pl.ds(pl.multiple_of((j // 4) * TX, TX), TX), :]
    to_terms(
        17, lambda q: x_v.at[pl.ds(pl.multiple_of((q // 4) * TX, TX), TX), :], trecv.at[5], 0
    )
    rest()

    arrived(13, drecv.at[2], ND)
    right_x = jnp.concatenate([drecv[2, q] for q in range(ND)], axis=0)
    start_st = start_v[pl.ds(i * 8, 8)].reshape(LANES, TILE)
    k20 = dot(k2, dot(kr1, k0, NN), NN)
    right = dot(k2, right_x, NTR) - dot(k20, start_st, NN)
    for g in range(8):
        right_o[:, g * TILE : (g + 1) * TILE] = right[g * BLOCK : (g + 1) * BLOCK]
    coef_o[0] = transposed(upper1)[:, :BLOCK]
    coef_o[1] = (p0 + r1)[:, :BLOCK]
    coef_o[2] = transposed(upper2)[:, :BLOCK]
    arrived(14, trecv.at[4], NT)
    left_u = jnp.concatenate([trecv[4, q] for q in range(NT)], axis=0)

    z = last()
    r2 = unpacked(z, 2)
    g3 = unpacked(z, 0) - dot(r2, jnp.concatenate([r2, pad], axis=0), NTR)
    upper3, inverse3 = factor(g3)
    arrived(17, trecv.at[5], NT)
    left_x = jnp.concatenate([trecv[5, q] for q in range(NT)], axis=0)
    left_x = left_x - dot(left_u, spread(r2), NTR)
    k3 = spread(inverse3)
    full = dot(k3, left_x, NTR)
    for m in range(4):
        tiles_two = full[m * 32 : (m + 1) * 32]

        @pl.when(lax.rem(j, 4) == m)
        def _():
            left_o[:, 0:TILE] = tiles_two[0:BLOCK]
            left_o[:, TILE : 2 * TILE] = tiles_two[BLOCK : 2 * BLOCK]

    coef_o[3] = (p02 + r2)[:, :BLOCK]
    coef_o[4] = transposed(upper3)[:, :BLOCK]
    for n, part in pending:
        pltpu.make_async_copy(part, part, send_sem.at[n]).wait()


def on_device(tiles, tile_rows, tile_cols, counts, start_block):
    smem = pl.BlockSpec(memory_space=pltpu.SMEM)
    anywhere = pl.BlockSpec(memory_space=pl.ANY)
    vmem = pl.BlockSpec(memory_space=pltpu.VMEM)
    return pl.pallas_call(
        kernel,
        out_shape=(
            jax.ShapeDtypeStruct((BLOCK, DOC_TILES * TILE // NT), F32),
            jax.ShapeDtypeStruct((BLOCK, TERM_TILES * TILE // ND), F32),
            jax.ShapeDtypeStruct((5, BLOCK, BLOCK), F32),
        ),
        in_specs=[smem, smem, smem, anywhere, anywhere],
        out_specs=(vmem, vmem, vmem),
        scratch_shapes=[
            pltpu.VMEM((SLOTS, TILE, TILE), BF16),
            pltpu.VMEM((TERM_TILES, BLOCK, TILE), F32),
            pltpu.VMEM((DOC_TILES * BLOCK, NT * LANES), BF16),
            pltpu.VMEM((TERM_TILES * BLOCK, ND * LANES), BF16),
            pltpu.VMEM((NT, 16, LANES), F32),
            pltpu.VMEM((ND, 16, LANES), F32),
            pltpu.VMEM((ND, SLOTS, TILE), F32),
            pltpu.VMEM((4, NT, TX, LANES), F32),
            pltpu.VMEM((6, NT, TX, LANES), F32),
            pltpu.VMEM((2, ND, DX, LANES), F32),
            pltpu.VMEM((3, ND, DX, LANES), F32),
            pltpu.VMEM((3, ND, 8, LANES), F32),
            pltpu.VMEM((3, NT, 8, LANES), F32),
            pltpu.VMEM((TILE, LANES), F32),
            pltpu.VMEM((TGROUPS, LANES, LANES), F32),
            pltpu.VMEM((TGROUPS * DX, LANES), F32),
            pltpu.VMEM((DGROUPS, TX, LANES), F32),
            pltpu.VMEM((TILE, LANES), F32),
            pltpu.SemaphoreType.DMA((SLOTS + 1,)),
            pltpu.SemaphoreType.DMA((18,)),
            pltpu.SemaphoreType.DMA((18,)),
        ],
        compiler_params=pltpu.CompilerParams(
            collective_id=0, has_side_effects=True, vmem_limit_bytes=60 * 1024 * 1024
        ),
    )(
        tile_rows.reshape(SLOTS),
        tile_cols.reshape(SLOTS),
        counts.reshape(1),
        tiles.reshape(SLOTS, TILE, TILE),
        start_block,
    )


def solution(mesh):
    return jax.shard_map(
        on_device,
        mesh=mesh,
        in_specs=(
            P("doc", "term", None, None, None),
            P("doc", "term", None),
            P("doc", "term", None),
            P("doc", "term"),
            P(None, "term"),
        ),
        out_specs=(P(None, ("doc", "term")), P(None, ("term", "doc")), P()),
        check_vma=False,
    )
```

```python
import functools

import jax
import jax.numpy as jnp
from jax import lax
from jax.experimental import pallas as pl
from jax.experimental.pallas import tpu as pltpu
from jax.sharding import PartitionSpec as P

MESH = pl.DeviceIdType.MESH
F32 = jnp.float32
BF16 = jnp.bfloat16
TILE = 512
BLOCK = 16
SLOTS = 8
LANES = SLOTS * BLOCK
TERM_TILES = 64
DOC_TILES = 32
ND = 8
NT = 16
DX = TILE // ND
TX = TILE // NT
DGROUPS = DOC_TILES * BLOCK // LANES
TGROUPS = TERM_TILES * BLOCK // LANES
N_DOCS = ND * DOC_TILES * TILE
N_TERMS = NT * TERM_TILES * TILE
HIGHEST = lax.Precision.HIGHEST


def dot(a, b, contract, precision=HIGHEST):
    return lax.dot_general(
        a, b, (contract, ((), ())), precision=precision, preferred_element_type=F32
    )


NN = ((1,), (0,))
NTR = ((1,), (1,))
TN = ((0,), (0,))


def halves(x):
    hi = x.astype(BF16)
    lo = (x - hi.astype(F32)).astype(BF16)
    return jnp.concatenate([hi, lo], axis=0)


def by_onehot(x, onehot, contract):
    n = x.shape[0]
    both = dot(halves(x), onehot, contract, None)
    return both[:n] + both[n:]


def iota(shape, dim):
    return lax.broadcasted_iota(jnp.int32, shape, dim)


def roll(x, shift):
    return pltpu.roll(x, shift, 1)


def fold(t):
    same = iota((LANES, LANES), 0) // BLOCK == iota((LANES, LANES), 1) // BLOCK
    t = jnp.where(same, t, 0.0)
    w = t[0:BLOCK]
    for g in range(1, SLOTS):
        w = w + t[g * BLOCK : (g + 1) * BLOCK]
    w = w + roll(w, 64)
    w = w + roll(w, 32)
    return w + roll(w, 16)


def packed(s, r):
    group = iota((8, LANES), 1) // BLOCK
    z = jnp.where(group == 0, s[0:8], s[8:16])
    if r is None:
        return z
    return jnp.where(group < 2, z, jnp.where(group == 2, r[0:8], r[8:16]))


def unpacked(z, first):
    lane = iota((BLOCK, LANES), 1)
    top = z if first == 0 else roll(z, LANES - BLOCK * first)
    low = roll(z, LANES - BLOCK * (first + 1))
    return jnp.where(lane < BLOCK, jnp.concatenate([top, low], axis=0), 0.0)


def spread(m):
    same = iota((LANES, LANES), 0) // BLOCK == iota((LANES, LANES), 1) // BLOCK
    r = m + roll(m, 16)
    r = r + roll(r, 32)
    r = r + roll(r, 64)
    return jnp.where(same, jnp.concatenate([r] * SLOTS, axis=0), 0.0)


def factor(s):
    lane = iota((BLOCK, LANES), 1)
    sub = iota((BLOCK, LANES), 0)
    m = jnp.where(lane < BLOCK, s, jnp.where(lane == sub + BLOCK, 1.0, 0.0))
    for c in range(BLOCK - 1):
        ratio = m[c : c + 1, :] / m[c : c + 1, c : c + 1]
        m = m - jnp.where(sub > c, m[:, c : c + 1], 0.0) * ratio
    diag = jnp.sum(jnp.where(lane == sub, m, 0.0), axis=1, keepdims=True)
    m = m * lax.rsqrt(diag)
    upper = jnp.where((lane < BLOCK) & (lane >= sub), m, 0.0)
    inverse = jnp.where(lane < BLOCK, roll(m, LANES - BLOCK), 0.0)
    return upper, inverse


def transposed(m):
    full = jnp.concatenate([m, jnp.zeros((LANES - BLOCK, LANES), F32)], axis=0)
    return full.T[:BLOCK, :]


def kernel(
    cnt_h, rows_h, cols_h, tiles_h, start_h,
    left_o, right_o, coef_o,
    cnt_s, rows_s, cols_s, tiles_v, start_v, st_v, sd_v,
    m1_v, d1_v, cs_v,
    tsend, trecv, dsend, drecv, za, zb,
    slots_v, share_v, cst_v, f0_v, x2_v,
    load_sem, send_sem, recv_sem,
):
    i = lax.axis_index("doc")
    j = lax.axis_index("term")
    bar = pltpu.get_barrier_semaphore()
    for d in range(1, NT):
        pl.semaphore_signal(bar, 1, device_id=(i, lax.rem(j + d, NT)), device_id_type=MESH)
    for d in range(1, ND):
        pl.semaphore_signal(bar, 1, device_id=(lax.rem(i + d, ND), j), device_id_type=MESH)

    def load_start(t, carry):
        columns = pl.ds(pl.multiple_of(t * TILE, TILE), TILE)
        pltpu.make_async_copy(start_h.at[:, columns], start_v.at[t], load_sem.at[SLOTS]).start()
        return carry

    lax.fori_loop(0, TERM_TILES, load_start, 0)
    rows_load = pltpu.make_async_copy(rows_h, rows_s, load_sem.at[SLOTS + 1])
    cols_load = pltpu.make_async_copy(cols_h, cols_s, load_sem.at[SLOTS + 2])
    cnt_load = pltpu.make_async_copy(cnt_h, cnt_s, load_sem.at[SLOTS + 3])
    cnt_load.start()
    rows_load.start()
    cols_load.start()
    loads = []
    for k in range(SLOTS):
        load = pltpu.make_async_copy(tiles_h.at[k], tiles_v.at[k], load_sem.at[k])
        load.start()
        loads.append(load)

    pending = []

    def to_terms(n, src_of, dst):
        def send(d, carry):
            q = lax.rem(j + d, NT)
            pltpu.make_async_remote_copy(
                src_ref=src_of(q), dst_ref=dst.at[j],
                send_sem=send_sem.at[n], recv_sem=recv_sem.at[n],
                device_id=(i, q), device_id_type=MESH,
            ).start()
            return carry
        lax.fori_loop(1, NT, send, 0)
        pending.append((n, dst.at[pl.ds(0, NT - 1)]))

    def to_docs(n, src_of, dst):
        def send(d, carry):
            q = lax.rem(i + d, ND)
            pltpu.make_async_remote_copy(
                src_ref=src_of(q), dst_ref=dst.at[i],
                send_sem=send_sem.at[n], recv_sem=recv_sem.at[n],
                device_id=(q, j), device_id_type=MESH,
            ).start()
            return carry
        lax.fori_loop(1, ND, send, 0)
        pending.append((n, dst.at[pl.ds(0, ND - 1)]))

    def arrived(n, dst, peers):
        part = dst.at[pl.ds(0, peers - 1)]
        pltpu.make_async_copy(part, part, recv_sem.at[n]).wait()

    def term_exchange(n, slot, total):
        for q in range(NT):
            tsend[slot, q] = total[q * TX : (q + 1) * TX]
        trecv[slot, j] = tsend[slot, j]
        to_terms(n, lambda q: tsend.at[slot, q], trecv.at[slot])

    def doc_exchange(n, slot, total):
        for q in range(ND):
            dsend[slot, q] = total[q * DX : (q + 1) * DX]
        drecv[slot, i] = dsend[slot, i]
        to_docs(n, lambda q: dsend.at[slot, q], drecv.at[slot])

    def forward_product(x):
        lane_slot = iota((TILE, LANES), 1) // BLOCK
        total = None
        for k in range(SLOTS):
            masked = [jnp.where(lane_slot == k, part, 0.0).astype(BF16) for part in x]
            weights = masked[0] if len(masked) == 1 else jnp.concatenate(masked, axis=1)
            part = dot(tiles_v[k], weights, NN, None)
            total = part if total is None else total + part
        if len(x) == 2:
            total = total[:, :LANES] + total[:, LANES:]
        return total

    def split(x):
        hi = x.astype(BF16).astype(F32)
        return [hi, x - hi]

    def stacked(x, groups):
        return jnp.concatenate([x[:, g * LANES : (g + 1) * LANES] for g in range(groups)], axis=0)

    def flat_of(x, groups):
        n = x.shape[0] // groups
        return jnp.concatenate([x[g * n : (g + 1) * n] for g in range(groups)], axis=1)

    def term_sum(slot):
        flat = jnp.concatenate([trecv[slot, q] for q in range(NT)], axis=1)
        return by_onehot(flat, st_v[...], NTR)

    def all_sum(n, base, z):
        za[n, i] = z
        to_docs(base, lambda q: za.at[n, i], za.at[n])

        def rest():
            arrived(base, za.at[n], ND)
            s = za[n, 0]
            for q in range(1, ND):
                s = s + za[n, q]
            zb[n, j] = s
            to_terms(base + 1, lambda q: zb.at[n, j], zb.at[n])

        def last():
            arrived(base + 1, zb.at[n], NT)
            s = zb[n, 0]
            for q in range(1, NT):
                s = s + zb[n, q]
            return s

        return rest, last

    pltpu.make_async_copy(start_v, start_v, load_sem.at[SLOTS]).wait()
    acc = jnp.zeros((2 * LANES, 2 * LANES), F32)
    for ch in range(8):
        both = halves(start_v[ch * 8 : (ch + 1) * 8].reshape(LANES, TILE))
        acc = acc + dot(both, both, NTR, None)
    t = acc[:LANES, :LANES] + acc[:LANES, LANES:] + acc[LANES:, :LANES] + acc[LANES:, LANES:]
    start_gram = packed(fold(t) * (1.0 / N_TERMS), None)

    cnt_load.wait()
    rows_load.wait()
    cols_load.wait()
    lane8 = iota((8, LANES), 1)
    sub8 = iota((8, LANES), 0)
    cnt = cnt_s[0, 0]
    row_at = jnp.zeros((8, LANES), jnp.int32)
    my_col = jnp.zeros((8, LANES), jnp.int32)
    col_of = jnp.zeros((8, LANES), jnp.int32)
    for k in range(SLOTS):
        here = lane8 // BLOCK == k
        row_at = jnp.where(here, rows_s[0, k] * BLOCK, row_at)
        my_col = jnp.where(here, cols_s[0, k], my_col)
        col_of = jnp.where(sub8 == k, cols_s[0, k], col_of)
    row_at = jnp.where(lane8 // BLOCK < cnt, row_at, -100000)
    my_col = jnp.where(lane8 // BLOCK < cnt, my_col, -10000)
    col_of = jnp.where(sub8 < cnt, col_of, -10000)
    col_at = my_col * BLOCK
    row_at = (row_at + lane8 % BLOCK).astype(F32)
    col_at = (col_at + lane8 % BLOCK).astype(F32)
    my_col = my_col.astype(F32)
    d1_v[i] = jnp.concatenate([col_of.astype(F32), col_at], axis=0)
    m1_v[j] = jnp.concatenate([start_gram, row_at], axis=0)

    col_sums = jnp.zeros((16, TILE), F32)
    for k in range(SLOTS):
        loads[k].wait()
        ones = jnp.where(iota((16, TILE), 0) == k, 1.0, 0.0).astype(BF16)
        col_sums = col_sums + dot(ones, tiles_v[k], NN, None)
    cs_v[i] = col_sums[:SLOTS]

    pl.semaphore_wait(bar, ND - 1 + NT - 1)
    to_docs(0, lambda q: d1_v.at[i], d1_v)
    to_docs(1, lambda q: cs_v.at[i], cs_v)
    to_terms(2, lambda q: m1_v.at[j], m1_v)

    term_exchange(3, 0, forward_product([jnp.ones((TILE, LANES), F32)]))
    slots_t = jnp.concatenate([start_v[cols_s[0, k]] for k in range(SLOTS)], axis=0).T
    slots_v[...] = slots_t

    arrived(0, d1_v, ND)
    arrived(1, cs_v, ND)
    cols_in = jnp.concatenate([d1_v[q, 0:8, :] for q in range(ND)], axis=0)
    sums_t = jnp.concatenate([cs_v[q] for q in range(ND)], axis=0).T
    cst_v[...] = sums_t
    same_col = jnp.where(cols_in == my_col[0:1, :], 1.0, 0.0)
    col_scale = lax.rsqrt(dot(sums_t, same_col, NN) + 1.0)
    scaled_slots = slots_v[...] * col_scale
    arrived(2, m1_v, NT)
    gram = m1_v[0, 0:8, :]
    for q in range(1, NT):
        gram = gram + m1_v[q, 0:8, :]
    _, inverse0 = factor(unpacked(gram, 0))
    k0 = spread(inverse0)
    term_exchange(4, 1, forward_product([dot(scaled_slots, k0, NTR)]))

    for q in range(NT):
        hit = iota((DOC_TILES * BLOCK, LANES), 0).astype(F32) == m1_v[q, 8:9, :]
        st_v[:, q * LANES : (q + 1) * LANES] = jnp.where(hit, 1.0, 0.0).astype(BF16)
    arrived(3, trecv.at[0], NT)
    row_scale = lax.rsqrt(term_sum(0) + 1.0)
    row_square = row_scale * row_scale

    arrived(4, trecv.at[1], NT)
    image = term_sum(1)
    wide = by_onehot(image * row_square, st_v[...], NN)
    for q in range(NT):
        tsend[2, q] = wide[:, q * LANES : (q + 1) * LANES]
    trecv[2, j] = tsend[2, j]
    to_terms(5, lambda q: tsend.at[2, q], trecv.at[2])
    f0 = stacked(image * row_scale, DGROUPS)
    rest, last = all_sum(0, 6, packed(fold(dot(f0, f0, TN)) * (1.0 / N_DOCS), None))
    for g in range(DGROUPS):
        f0_v[g] = f0[g * TX : (g + 1) * TX]
    trecv[4, j] = f0_v[j // 4]
    to_terms(8, lambda q: f0_v.at[q // 4], trecv.at[4])

    for q in range(ND):
        hit = iota((TERM_TILES * BLOCK, LANES), 0).astype(F32) == d1_v[q, 8:9, :]
        sd_v[:, q * LANES : (q + 1) * LANES] = jnp.where(hit, 1.0, 0.0).astype(BF16)
    rest()
    arrived(5, trecv.at[2], NT)
    pieces = jnp.concatenate([trecv[2, q] for q in range(NT)], axis=0).T
    hi = pieces.astype(BF16)
    lo = (pieces - hi.astype(F32)).astype(BF16)
    back = []
    for k in range(SLOTS):
        cut = slice(k * BLOCK, (k + 1) * BLOCK)
        both = dot(jnp.concatenate([hi[cut], lo[cut]], axis=0), tiles_v[k], NN, None)
        back.append(both[:BLOCK] + both[BLOCK:])
    doc_exchange(9, 0, jnp.concatenate(back, axis=0).T)

    cols_wide = jnp.concatenate([cols_in] * TGROUPS, axis=1)
    tile_at = (iota((ND * SLOTS, TERM_TILES * BLOCK), 1) // BLOCK).astype(F32)
    my_sums = cst_v[pl.ds(pl.multiple_of(i * DX, DX), DX), :]
    col_share = lax.rsqrt(dot(my_sums, jnp.where(cols_wide == tile_at, 1.0, 0.0), NN) + 1.0)
    col_square = col_share * col_share
    window = pl.ds(pl.multiple_of(128 * (i // 2), 128), 128)
    for g in range(TGROUPS):
        share_v[g] = start_v[g * 8 : (g + 1) * 8, :, window].reshape(LANES, 128).T
    half = pl.multiple_of(DX * lax.rem(i, 2), DX)
    start_share = jnp.concatenate([share_v[g, pl.ds(half, DX), :] for g in range(TGROUPS)], axis=0)
    e_share = dot(start_share, k0, NTR)
    upper1, inverse1 = factor(unpacked(last(), 0))
    k1 = spread(inverse1)
    p0 = upper1 * (N_DOCS / N_TERMS)
    expected = dot(e_share, spread(p0), NTR)
    u1 = dot(f0, k1, NTR)

    arrived(9, drecv.at[0], ND)
    flat = jnp.concatenate([drecv[0, q] for q in range(ND)], axis=1)
    image = by_onehot(flat, sd_v[...], NTR)
    wide = by_onehot(image * col_square, sd_v[...], NN)
    for q in range(ND):
        dsend[1, q] = wide[:, q * LANES : (q + 1) * LANES]
    drecv[1, i] = dsend[1, i]
    to_docs(10, lambda q: dsend.at[1, q], drecv.at[1])
    b1 = dot(stacked(image * col_share, TGROUPS), k1, NTR) - expected
    t2 = dot(b1, jnp.concatenate([b1, e_share], axis=1), TN) * (1.0 / N_TERMS)
    rest, last = all_sum(1, 11, packed(fold(t2[:, :LANES]), fold(t2[:, LANES:])))
    for g in range(TGROUPS):
        share_v[g, 0:DX, :] = b1[g * DX : (g + 1) * DX]
    drecv[2, i] = share_v[i, 0:DX, :]
    to_docs(13, lambda q: share_v.at[q, pl.ds(0, DX), :], drecv.at[2])

    arrived(10, drecv.at[1], ND)
    pieces = jnp.concatenate([drecv[1, q] for q in range(ND)], axis=0)
    term_exchange(14, 3, forward_product(split(pieces)))
    rest()
    z = last()
    r1 = unpacked(z, 2)
    pad = jnp.zeros((LANES - BLOCK, LANES), F32)
    g2 = unpacked(z, 0) - dot(r1, jnp.concatenate([r1, pad], axis=0), NTR)
    upper2, inverse2 = factor(g2)
    k2 = spread(inverse2)
    kr1 = spread(r1)
    p02 = upper2 * (N_TERMS / N_DOCS)
    k21 = dot(k2, k1, NN)
    known = dot(k2, spread(p0 + r1), NN) + dot(spread(p02), k1, NN)
    expected = dot(f0, known, NTR)

    arrived(14, trecv.at[3], NT)
    image = term_sum(3) * row_scale
    x2 = dot(stacked(image, DGROUPS), k21, NTR) - expected
    t3 = dot(x2, jnp.concatenate([x2, u1], axis=1), TN) * (1.0 / N_DOCS)
    rest, last = all_sum(2, 15, packed(fold(t3[:, :LANES]), fold(t3[:, LANES:])))
    for g in range(DGROUPS):
        x2_v[g] = x2[g * TX : (g + 1) * TX]
    trecv[5, j] = x2_v[j // 4]
    to_terms(17, lambda q: x2_v.at[q // 4], trecv.at[5])
    arrived(13, drecv.at[2], ND)
    right_x = jnp.concatenate([drecv[2, q] for q in range(ND)], axis=0)
    rest()

    start_st = start_v[pl.ds(i * 8, 8)].reshape(LANES, TILE)
    k20 = dot(k2, dot(kr1, k0, NN), NN)
    right = dot(k2, right_x, NTR) - dot(k20, start_st, NN)
    for g in range(8):
        right_o[:, g * TILE : (g + 1) * TILE] = right[g * BLOCK : (g + 1) * BLOCK]
    coef_o[0] = transposed(upper1)[:, :BLOCK]
    coef_o[1] = (p0 + r1)[:, :BLOCK]
    coef_o[2] = transposed(upper2)[:, :BLOCK]
    arrived(8, trecv.at[4], NT)
    left_u = dot(jnp.concatenate([trecv[4, q] for q in range(NT)], axis=0), k1, NTR)
    arrived(17, trecv.at[5], NT)
    left_x = jnp.concatenate([trecv[5, q] for q in range(NT)], axis=0)

    z = last()
    r2 = unpacked(z, 2)
    g3 = unpacked(z, 0) - dot(r2, jnp.concatenate([r2, pad], axis=0), NTR)
    upper3, inverse3 = factor(g3)
    left_x = left_x - dot(left_u, spread(r2), NTR)
    rep = inverse3 + roll(inverse3, 16)
    rep = rep + roll(rep, 32)
    rep = rep + roll(rep, 64)
    mine = iota((2 * BLOCK, LANES), 1) // BLOCK == iota((2 * BLOCK, LANES), 0) // BLOCK + 2 * lax.rem(j, 4)
    left = dot(jnp.where(mine, jnp.concatenate([rep, rep], axis=0), 0.0), left_x, NTR)
    left_o[:, 0:TILE] = left[0:BLOCK]
    left_o[:, TILE : 2 * TILE] = left[BLOCK : 2 * BLOCK]
    coef_o[3] = (p02 + r2)[:, :BLOCK]
    coef_o[4] = transposed(upper3)[:, :BLOCK]
    for n, part in pending:
        pltpu.make_async_copy(part, part, send_sem.at[n]).wait()


def hand_over(left_i, right_i, coef_i, left_o, right_o, coef_o):
    left_o[...] = left_i[...]
    right_o[...] = right_i[...]
    coef_o[...] = coef_i[...]


def on_device(tiles, tile_rows, tile_cols, counts, start_block):
    anywhere = pl.BlockSpec(memory_space=pl.ANY)
    vmem = pl.BlockSpec(memory_space=pltpu.VMEM)
    shapes = (
        jax.ShapeDtypeStruct((BLOCK, DOC_TILES * TILE // NT), F32),
        jax.ShapeDtypeStruct((BLOCK, TERM_TILES * TILE // ND), F32),
        jax.ShapeDtypeStruct((5, BLOCK, BLOCK), F32),
    )
    results = pl.pallas_call(
        kernel,
        out_shape=shapes,
        in_specs=[anywhere] * 5,
        out_specs=(vmem, vmem, vmem),
        scratch_shapes=[
            pltpu.SMEM((1, 1), jnp.int32),
            pltpu.SMEM((1, SLOTS), jnp.int32),
            pltpu.SMEM((1, SLOTS), jnp.int32),
            pltpu.VMEM((SLOTS, TILE, TILE), BF16),
            pltpu.VMEM((TERM_TILES, BLOCK, TILE), F32),
            pltpu.VMEM((DOC_TILES * BLOCK, NT * LANES), BF16),
            pltpu.VMEM((TERM_TILES * BLOCK, ND * LANES), BF16),
            pltpu.VMEM((NT, 16, LANES), F32),
            pltpu.VMEM((ND, 16, LANES), F32),
            pltpu.VMEM((ND, SLOTS, TILE), F32),
            pltpu.VMEM((4, NT, TX, LANES), F32),
            pltpu.VMEM((6, NT, TX, LANES), F32),
            pltpu.VMEM((2, ND, DX, LANES), F32),
            pltpu.VMEM((3, ND, DX, LANES), F32),
            pltpu.VMEM((3, ND, 8, LANES), F32),
            pltpu.VMEM((3, NT, 8, LANES), F32),
            pltpu.VMEM((TILE, LANES), F32),
            pltpu.VMEM((TGROUPS, LANES, LANES), F32),
            pltpu.VMEM((TILE, ND * SLOTS), F32),
            pltpu.VMEM((DGROUPS, TX, LANES), F32),
            pltpu.VMEM((DGROUPS, TX, LANES), F32),
            pltpu.SemaphoreType.DMA((SLOTS + 4,)),
            pltpu.SemaphoreType.DMA((18,)),
            pltpu.SemaphoreType.DMA((18,)),
        ],
        compiler_params=pltpu.CompilerParams(
            collective_id=0, has_side_effects=True, vmem_limit_bytes=65000000
        ),
    )(
        counts,
        tile_rows.reshape(1, SLOTS),
        tile_cols.reshape(1, SLOTS),
        tiles.reshape(SLOTS, TILE, TILE),
        start_block,
    )
    return pl.pallas_call(
        hand_over,
        out_shape=shapes,
        in_specs=[vmem, vmem, vmem],
        out_specs=(vmem, vmem, vmem),
        compiler_params=pltpu.CompilerParams(vmem_limit_bytes=8 * 1024 * 1024),
    )(*results)


def solution(mesh):
    return jax.shard_map(
        on_device,
        mesh=mesh,
        in_specs=(
            P("doc", "term", None, None, None),
            P("doc", "term", None),
            P("doc", "term", None),
            P("doc", "term"),
            P(None, "term"),
        ),
        out_specs=(P(None, ("doc", "term")), P(None, ("term", "doc")), P()),
        check_vma=False,
    )
```

```python
import functools

import jax
import jax.numpy as jnp
from jax import lax
from jax.experimental import pallas as pl
from jax.experimental.pallas import tpu as pltpu
from jax.sharding import PartitionSpec as P

MESH = pl.DeviceIdType.MESH
F32 = jnp.float32
BF16 = jnp.bfloat16
TILE = 512
BLOCK = 16
SLOTS = 8
LANES = SLOTS * BLOCK
TERM_TILES = 64
DOC_TILES = 32
ND = 8
NT = 16
DX = TILE // ND
TX = TILE // NT
DGROUPS = DOC_TILES * BLOCK // LANES
TGROUPS = TERM_TILES * BLOCK // LANES
N_DOCS = ND * DOC_TILES * TILE
N_TERMS = NT * TERM_TILES * TILE
HIGHEST = lax.Precision.HIGHEST


def dot(a, b, contract, precision=HIGHEST):
    return lax.dot_general(
        a, b, (contract, ((), ())), precision=precision, preferred_element_type=F32
    )


NN = ((1,), (0,))
NTR = ((1,), (1,))
TN = ((0,), (0,))


def halves(x):
    hi = x.astype(BF16)
    lo = (x - hi.astype(F32)).astype(BF16)
    return jnp.concatenate([hi, lo], axis=0)


def by_onehot(x, onehot, contract):
    n = x.shape[0]
    both = dot(halves(x), onehot, contract, None)
    return both[:n] + both[n:]


def iota(shape, dim):
    return lax.broadcasted_iota(jnp.int32, shape, dim)


def roll(x, shift):
    return pltpu.roll(x, shift, 1)


def fold(t):
    same = iota((LANES, LANES), 0) // BLOCK == iota((LANES, LANES), 1) // BLOCK
    t = jnp.where(same, t, 0.0)
    w = t[0:BLOCK]
    for g in range(1, SLOTS):
        w = w + t[g * BLOCK : (g + 1) * BLOCK]
    w = w + roll(w, 64)
    w = w + roll(w, 32)
    return w + roll(w, 16)


def packed(s, r):
    group = iota((8, LANES), 1) // BLOCK
    z = jnp.where(group == 0, s[0:8], s[8:16])
    if r is None:
        return z
    return jnp.where(group < 2, z, jnp.where(group == 2, r[0:8], r[8:16]))


def unpacked(z, first):
    lane = iota((BLOCK, LANES), 1)
    top = z if first == 0 else roll(z, LANES - BLOCK * first)
    low = roll(z, LANES - BLOCK * (first + 1))
    return jnp.where(lane < BLOCK, jnp.concatenate([top, low], axis=0), 0.0)


def spread(m):
    same = iota((LANES, LANES), 0) // BLOCK == iota((LANES, LANES), 1) // BLOCK
    r = m + roll(m, 16)
    r = r + roll(r, 32)
    r = r + roll(r, 64)
    return jnp.where(same, jnp.concatenate([r] * SLOTS, axis=0), 0.0)


def factor(s):
    lane = iota((BLOCK, LANES), 1)
    sub = iota((BLOCK, LANES), 0)
    m = jnp.where(lane < BLOCK, s, jnp.where(lane == sub + BLOCK, 1.0, 0.0))
    for c in range(BLOCK - 1):
        ratio = m[c : c + 1, :] / m[c : c + 1, c : c + 1]
        m = m - jnp.where(sub > c, m[:, c : c + 1], 0.0) * ratio
    diag = jnp.sum(jnp.where(lane == sub, m, 0.0), axis=1, keepdims=True)
    m = m * lax.rsqrt(diag)
    upper = jnp.where((lane < BLOCK) & (lane >= sub), m, 0.0)
    inverse = jnp.where(lane < BLOCK, roll(m, LANES - BLOCK), 0.0)
    return upper, inverse


def transposed(m):
    full = jnp.concatenate([m, jnp.zeros((LANES - BLOCK, LANES), F32)], axis=0)
    return full.T[:BLOCK, :]


def kernel(
    cnt_h, rows_h, cols_h, tiles_h, start_h,
    left_o, right_o, coef_o,
    cnt_s, rows_s, cols_s, tiles_v, start_v, st_v, sd_v,
    m1_v, d1_v, cs_v,
    tsend, trecv, dsend, drecv, za, zb,
    slots_v, share_v, cst_v, rs_v, rsr_v, rst_v, pk_v, pkr_v,
    load_sem, send_sem, recv_sem,
):
    i = lax.axis_index("doc")
    j = lax.axis_index("term")
    bar = pltpu.get_barrier_semaphore()
    for d in range(1, NT):
        pl.semaphore_signal(bar, 1, device_id=(i, lax.rem(j + d, NT)), device_id_type=MESH)
    for d in range(1, ND):
        pl.semaphore_signal(bar, 1, device_id=(lax.rem(i + d, ND), j), device_id_type=MESH)

    def load_start(t, carry):
        columns = pl.ds(pl.multiple_of(t * TILE, TILE), TILE)
        pltpu.make_async_copy(start_h.at[:, columns], start_v.at[t], load_sem.at[SLOTS]).start()
        return carry

    lax.fori_loop(0, TERM_TILES, load_start, 0)
    rows_load = pltpu.make_async_copy(rows_h, rows_s, load_sem.at[SLOTS + 1])
    cols_load = pltpu.make_async_copy(cols_h, cols_s, load_sem.at[SLOTS + 2])
    cnt_load = pltpu.make_async_copy(cnt_h, cnt_s, load_sem.at[SLOTS + 3])
    cnt_load.start()
    rows_load.start()
    cols_load.start()
    loads = []
    for k in range(SLOTS):
        load = pltpu.make_async_copy(tiles_h.at[k], tiles_v.at[k], load_sem.at[k])
        load.start()
        loads.append(load)

    pending = []

    def to_terms(n, src_of, dst):
        def send(d, carry):
            q = lax.rem(j + d, NT)
            pltpu.make_async_remote_copy(
                src_ref=src_of(q), dst_ref=dst.at[j],
                send_sem=send_sem.at[n], recv_sem=recv_sem.at[n],
                device_id=(i, q), device_id_type=MESH,
            ).start()
            return carry
        lax.fori_loop(1, NT, send, 0)
        pending.append((n, dst.at[pl.ds(0, NT - 1)]))

    def to_docs(n, src_of, dst):
        def send(d, carry):
            q = lax.rem(i + d, ND)
            pltpu.make_async_remote_copy(
                src_ref=src_of(q), dst_ref=dst.at[i],
                send_sem=send_sem.at[n], recv_sem=recv_sem.at[n],
                device_id=(q, j), device_id_type=MESH,
            ).start()
            return carry
        lax.fori_loop(1, ND, send, 0)
        pending.append((n, dst.at[pl.ds(0, ND - 1)]))

    def arrived(n, dst, peers):
        part = dst.at[pl.ds(0, peers - 1)]
        pltpu.make_async_copy(part, part, recv_sem.at[n]).wait()

    def term_exchange(n, slot, total):
        for q in range(NT):
            tsend[slot, q] = total[q * TX : (q + 1) * TX]
        trecv[slot, j] = tsend[slot, j]
        to_terms(n, lambda q: tsend.at[slot, q], trecv.at[slot])

    def doc_exchange(n, slot, total):
        for q in range(ND):
            dsend[slot, q] = total[q * DX : (q + 1) * DX]
        drecv[slot, i] = dsend[slot, i]
        to_docs(n, lambda q: dsend.at[slot, q], drecv.at[slot])

    def forward_product(x):
        lane_slot = iota((TILE, LANES), 1) // BLOCK
        total = None
        for k in range(SLOTS):
            masked = [jnp.where(lane_slot == k, part, 0.0).astype(BF16) for part in x]
            weights = masked[0] if len(masked) == 1 else jnp.concatenate(masked, axis=1)
            part = dot(tiles_v[k], weights, NN, None)
            total = part if total is None else total + part
        if len(x) == 2:
            total = total[:, :LANES] + total[:, LANES:]
        return total

    def split(x):
        hi = x.astype(BF16).astype(F32)
        return [hi, x - hi]

    def stacked(x, groups):
        return jnp.concatenate([x[:, g * LANES : (g + 1) * LANES] for g in range(groups)], axis=0)

    def flat_of(x, groups):
        n = x.shape[0] // groups
        return jnp.concatenate([x[g * n : (g + 1) * n] for g in range(groups)], axis=1)

    def pack(x, out):
        group = iota((8, LANES), 1) // (2 * BLOCK)
        for g in range(DGROUPS):
            rows = [x[g * TX + 8 * h : g * TX + 8 * (h + 1)] for h in range(4)]
            for m in range(4):
                total = None
                for h in range(4):
                    shift = (32 * (h - m)) % LANES
                    turned = rows[h] if shift == 0 else roll(rows[h], shift)
                    total = turned if total is None else jnp.where(group == h, turned, total)
                out[4 * g + m] = total

    def unpack(ref):
        rows = []
        for q in range(NT):
            for h in range(4):
                rows.append(ref[q] if h == 0 else roll(ref[q], LANES - 32 * h))
        return jnp.concatenate(rows, axis=0)

    def term_sum(slot):
        flat = jnp.concatenate([trecv[slot, q] for q in range(NT)], axis=1)
        return by_onehot(flat, st_v[...], NTR)

    def all_sum(n, base, z):
        za[n, i] = z
        to_docs(base, lambda q: za.at[n, i], za.at[n])

        def rest():
            arrived(base, za.at[n], ND)
            s = za[n, 0]
            for q in range(1, ND):
                s = s + za[n, q]
            zb[n, j] = s
            to_terms(base + 1, lambda q: zb.at[n, j], zb.at[n])

        def last():
            arrived(base + 1, zb.at[n], NT)
            s = zb[n, 0]
            for q in range(1, NT):
                s = s + zb[n, q]
            return s

        return rest, last

    pltpu.make_async_copy(start_v, start_v, load_sem.at[SLOTS]).wait()
    acc = jnp.zeros((2 * LANES, 2 * LANES), F32)
    for ch in range(8):
        both = halves(start_v[ch * 8 : (ch + 1) * 8].reshape(LANES, TILE))
        acc = acc + dot(both, both, NTR, None)
    t = acc[:LANES, :LANES] + acc[:LANES, LANES:] + acc[LANES:, :LANES] + acc[LANES:, LANES:]
    start_gram = packed(fold(t) * (1.0 / N_TERMS), None)

    cnt_load.wait()
    rows_load.wait()
    cols_load.wait()
    lane8 = iota((8, LANES), 1)
    sub8 = iota((8, LANES), 0)
    cnt = cnt_s[0, 0]
    row_at = jnp.zeros((8, LANES), jnp.int32)
    my_col = jnp.zeros((8, LANES), jnp.int32)
    col_of = jnp.zeros((8, LANES), jnp.int32)
    row_of = jnp.zeros((8, LANES), jnp.int32)
    for k in range(SLOTS):
        here = lane8 // BLOCK == k
        row_at = jnp.where(here, rows_s[0, k] * BLOCK, row_at)
        my_col = jnp.where(here, cols_s[0, k], my_col)
        col_of = jnp.where(sub8 == k, cols_s[0, k], col_of)
        row_of = jnp.where(sub8 == k, rows_s[0, k], row_of)
    row_at = jnp.where(lane8 // BLOCK < cnt, row_at, -100000)
    my_col = jnp.where(lane8 // BLOCK < cnt, my_col, -10000)
    col_of = jnp.where(sub8 < cnt, col_of, -10000)
    row_of = jnp.where(sub8 < cnt, row_of, -10000)
    col_at = my_col * BLOCK
    row_at = (row_at + lane8 % BLOCK).astype(F32)
    col_at = (col_at + lane8 % BLOCK).astype(F32)
    my_col = my_col.astype(F32)
    d1_v[i] = jnp.concatenate([col_of.astype(F32), col_at], axis=0)
    m1_v[j] = jnp.concatenate([start_gram, row_at, row_of.astype(F32)], axis=0)

    col_sums = jnp.zeros((16, TILE), F32)
    for k in range(SLOTS):
        loads[k].wait()
        ones = jnp.where(iota((16, TILE), 0) == k, 1.0, 0.0).astype(BF16)
        col_sums = col_sums + dot(ones, tiles_v[k], NN, None)
    cs_v[i] = col_sums[:SLOTS]

    pl.semaphore_wait(bar, ND - 1 + NT - 1)
    to_docs(0, lambda q: d1_v.at[i], d1_v)
    to_docs(1, lambda q: cs_v.at[i], cs_v)
    to_terms(2, lambda q: m1_v.at[j], m1_v)

    row_sums = jnp.zeros((16, TILE), F32)
    for k in range(SLOTS):
        ones = jnp.where(iota((16, TILE), 0) == k, 1.0, 0.0).astype(BF16)
        row_sums = row_sums + dot(ones, tiles_v[k], NTR, None)
    for g in range(DGROUPS):
        rs_v[g] = row_sums[:SLOTS, g * LANES : (g + 1) * LANES]
    rsr_v[j] = rs_v[j // 4]
    to_terms(3, lambda q: rs_v.at[q // 4], rsr_v)
    slots_t = jnp.concatenate([start_v[cols_s[0, k]] for k in range(SLOTS)], axis=0).T
    slots_v[...] = slots_t

    arrived(0, d1_v, ND)
    arrived(1, cs_v, ND)
    cols_in = jnp.concatenate([d1_v[q, 0:8, :] for q in range(ND)], axis=0)
    sums_t = jnp.concatenate([cs_v[q] for q in range(ND)], axis=0).T
    cst_v[...] = sums_t
    same_col = jnp.where(cols_in == my_col[0:1, :], 1.0, 0.0)
    col_scale = lax.rsqrt(dot(sums_t, same_col, NN) + 1.0)
    scaled_slots = slots_v[...] * col_scale
    arrived(2, m1_v, NT)
    gram = m1_v[0, 0:8, :]
    for q in range(1, NT):
        gram = gram + m1_v[q, 0:8, :]
    _, inverse0 = factor(unpacked(gram, 0))
    k0 = spread(inverse0)
    term_exchange(4, 1, forward_product([dot(scaled_slots, k0, NTR)]))

    for q in range(NT):
        hit = iota((DOC_TILES * BLOCK, LANES), 0).astype(F32) == m1_v[q, 8:9, :]
        st_v[:, q * LANES : (q + 1) * LANES] = jnp.where(hit, 1.0, 0.0).astype(BF16)
    rows_in = jnp.concatenate([m1_v[q, 16:24, :] for q in range(NT)], axis=0)
    rows_wide = jnp.concatenate([rows_in] * DGROUPS, axis=1)
    row_tile = (iota((LANES, DOC_TILES * BLOCK), 1) // BLOCK).astype(F32)
    same_row = jnp.where(rows_wide == row_tile, 1.0, 0.0)
    arrived(3, rsr_v, NT)
    rst_v[...] = jnp.concatenate([rsr_v[q] for q in range(NT)], axis=0).T
    my_rows = rst_v[pl.ds(pl.multiple_of(TX * lax.rem(j, 4), TX), TX), :]
    row_scale = lax.rsqrt(dot(my_rows, same_row, NN) + 1.0)
    row_square = row_scale * row_scale

    arrived(4, trecv.at[1], NT)
    image = term_sum(1)
    wide = by_onehot(image * row_square, st_v[...], NN)
    for q in range(NT):
        tsend[2, q] = wide[:, q * LANES : (q + 1) * LANES]
    trecv[2, j] = tsend[2, j]
    to_terms(5, lambda q: tsend.at[2, q], trecv.at[2])
    f0 = stacked(image * row_scale, DGROUPS)
    rest, last = all_sum(0, 6, packed(fold(dot(f0, f0, TN)) * (1.0 / N_DOCS), None))
    pack(f0, pk_v.at[0])
    pkr_v[0, j] = pk_v[0, j]
    to_terms(8, lambda q: pk_v.at[0, q], pkr_v.at[0])

    for q in range(ND):
        hit = iota((TERM_TILES * BLOCK, LANES), 0).astype(F32) == d1_v[q, 8:9, :]
        sd_v[:, q * LANES : (q + 1) * LANES] = jnp.where(hit, 1.0, 0.0).astype(BF16)
    rest()
    arrived(5, trecv.at[2], NT)
    pieces = jnp.concatenate([trecv[2, q] for q in range(NT)], axis=0).T
    hi = pieces.astype(BF16)
    lo = (pieces - hi.astype(F32)).astype(BF16)
    back = []
    for k in range(SLOTS):
        cut = slice(k * BLOCK, (k + 1) * BLOCK)
        both = dot(jnp.concatenate([hi[cut], lo[cut]], axis=0), tiles_v[k], NN, None)
        back.append(both[:BLOCK] + both[BLOCK:])
    doc_exchange(9, 0, jnp.concatenate(back, axis=0).T)

    cols_wide = jnp.concatenate([cols_in] * TGROUPS, axis=1)
    tile_at = (iota((ND * SLOTS, TERM_TILES * BLOCK), 1) // BLOCK).astype(F32)
    my_sums = cst_v[pl.ds(pl.multiple_of(i * DX, DX), DX), :]
    col_share = lax.rsqrt(dot(my_sums, jnp.where(cols_wide == tile_at, 1.0, 0.0), NN) + 1.0)
    col_square = col_share * col_share
    window = pl.ds(pl.multiple_of(128 * (i // 2), 128), 128)
    for g in range(TGROUPS):
        share_v[g] = start_v[g * 8 : (g + 1) * 8, :, window].reshape(LANES, 128).T
    half = pl.multiple_of(DX * lax.rem(i, 2), DX)
    start_share = jnp.concatenate([share_v[g, pl.ds(half, DX), :] for g in range(TGROUPS)], axis=0)
    e_share = dot(start_share, k0, NTR)
    upper1, inverse1 = factor(unpacked(last(), 0))
    k1 = spread(inverse1)
    p0 = upper1 * (N_DOCS / N_TERMS)
    expected = dot(e_share, spread(p0), NTR)
    u1 = dot(f0, k1, NTR)

    arrived(9, drecv.at[0], ND)
    flat = jnp.concatenate([drecv[0, q] for q in range(ND)], axis=1)
    image = by_onehot(flat, sd_v[...], NTR)
    wide = by_onehot(image * col_square, sd_v[...], NN)
    for q in range(ND):
        dsend[1, q] = wide[:, q * LANES : (q + 1) * LANES]
    drecv[1, i] = dsend[1, i]
    to_docs(10, lambda q: dsend.at[1, q], drecv.at[1])
    b1 = dot(stacked(image * col_share, TGROUPS), k1, NTR) - expected
    t2 = dot(b1, jnp.concatenate([b1, e_share], axis=1), TN) * (1.0 / N_TERMS)
    rest, last = all_sum(1, 11, packed(fold(t2[:, :LANES]), fold(t2[:, LANES:])))
    for g in range(TGROUPS):
        share_v[g, 0:DX, :] = b1[g * DX : (g + 1) * DX]
    drecv[2, i] = share_v[i, 0:DX, :]
    to_docs(13, lambda q: share_v.at[q, pl.ds(0, DX), :], drecv.at[2])

    rest()
    arrived(10, drecv.at[1], ND)
    pieces = jnp.concatenate([drecv[1, q] for q in range(ND)], axis=0)
    term_exchange(14, 3, forward_product(split(pieces)))
    z = last()
    r1 = unpacked(z, 2)
    pad = jnp.zeros((LANES - BLOCK, LANES), F32)
    g2 = unpacked(z, 0) - dot(r1, jnp.concatenate([r1, pad], axis=0), NTR)
    upper2, inverse2 = factor(g2)
    k2 = spread(inverse2)
    kr1 = spread(r1)
    p02 = upper2 * (N_TERMS / N_DOCS)
    k21 = dot(k2, k1, NN)
    known = dot(k2, spread(p0 + r1), NN) + dot(spread(p02), k1, NN)
    expected = dot(f0, known, NTR)

    arrived(14, trecv.at[3], NT)
    image = term_sum(3) * row_scale
    x2 = dot(stacked(image, DGROUPS), k21, NTR) - expected
    t3 = dot(x2, jnp.concatenate([x2, u1], axis=1), TN) * (1.0 / N_DOCS)
    rest, last = all_sum(2, 15, packed(fold(t3[:, :LANES]), fold(t3[:, LANES:])))
    pack(x2, pk_v.at[1])
    pkr_v[1, j] = pk_v[1, j]
    to_terms(17, lambda q: pk_v.at[1, q], pkr_v.at[1])
    arrived(13, drecv.at[2], ND)
    right_x = jnp.concatenate([drecv[2, q] for q in range(ND)], axis=0)
    rest()

    start_st = start_v[pl.ds(i * 8, 8)].reshape(LANES, TILE)
    k20 = dot(k2, dot(kr1, k0, NN), NN)
    right = dot(k2, right_x, NTR) - dot(k20, start_st, NN)
    for g in range(8):
        right_o[:, g * TILE : (g + 1) * TILE] = right[g * BLOCK : (g + 1) * BLOCK]
    coef_o[0] = transposed(upper1)[:, :BLOCK]
    coef_o[1] = (p0 + r1)[:, :BLOCK]
    coef_o[2] = transposed(upper2)[:, :BLOCK]
    arrived(8, pkr_v.at[0], NT)
    left_u = dot(unpack(pkr_v.at[0]), k1, NTR)
    arrived(17, pkr_v.at[1], NT)
    left_x = unpack(pkr_v.at[1])

    z = last()
    r2 = unpacked(z, 2)
    g3 = unpacked(z, 0) - dot(r2, jnp.concatenate([r2, pad], axis=0), NTR)
    upper3, inverse3 = factor(g3)
    left_x = left_x - dot(left_u, spread(r2), NTR)
    rep = inverse3 + roll(inverse3, 16)
    rep = rep + roll(rep, 32)
    rep = rep + roll(rep, 64)
    mine = iota((2 * BLOCK, LANES), 1) // BLOCK == iota((2 * BLOCK, LANES), 0) // BLOCK
    left = dot(jnp.where(mine, jnp.concatenate([rep, rep], axis=0), 0.0), left_x, NTR)
    left_o[:, 0:TILE] = left[0:BLOCK]
    left_o[:, TILE : 2 * TILE] = left[BLOCK : 2 * BLOCK]
    coef_o[3] = (p02 + r2)[:, :BLOCK]
    coef_o[4] = transposed(upper3)[:, :BLOCK]
    for n, part in pending:
        pltpu.make_async_copy(part, part, send_sem.at[n]).wait()


def hand_over(left_i, right_i, coef_i, left_o, right_o, coef_o):
    left_o[...] = left_i[...]
    right_o[...] = right_i[...]
    coef_o[...] = coef_i[...]


def on_device(tiles, tile_rows, tile_cols, counts, start_block):
    anywhere = pl.BlockSpec(memory_space=pl.ANY)
    vmem = pl.BlockSpec(memory_space=pltpu.VMEM)
    shapes = (
        jax.ShapeDtypeStruct((BLOCK, DOC_TILES * TILE // NT), F32),
        jax.ShapeDtypeStruct((BLOCK, TERM_TILES * TILE // ND), F32),
        jax.ShapeDtypeStruct((5, BLOCK, BLOCK), F32),
    )
    results = pl.pallas_call(
        kernel,
        out_shape=shapes,
        in_specs=[anywhere] * 5,
        out_specs=(vmem, vmem, vmem),
        scratch_shapes=[
            pltpu.SMEM((1, 1), jnp.int32),
            pltpu.SMEM((1, SLOTS), jnp.int32),
            pltpu.SMEM((1, SLOTS), jnp.int32),
            pltpu.VMEM((SLOTS, TILE, TILE), BF16),
            pltpu.VMEM((TERM_TILES, BLOCK, TILE), F32),
            pltpu.VMEM((DOC_TILES * BLOCK, NT * LANES), BF16),
            pltpu.VMEM((TERM_TILES * BLOCK, ND * LANES), BF16),
            pltpu.VMEM((NT, 24, LANES), F32),
            pltpu.VMEM((ND, 16, LANES), F32),
            pltpu.VMEM((ND, SLOTS, TILE), F32),
            pltpu.VMEM((4, NT, TX, LANES), F32),
            pltpu.VMEM((4, NT, TX, LANES), F32),
            pltpu.VMEM((2, ND, DX, LANES), F32),
            pltpu.VMEM((3, ND, DX, LANES), F32),
            pltpu.VMEM((3, ND, 8, LANES), F32),
            pltpu.VMEM((3, NT, 8, LANES), F32),
            pltpu.VMEM((TILE, LANES), F32),
            pltpu.VMEM((TGROUPS, LANES, LANES), F32),
            pltpu.VMEM((TILE, ND * SLOTS), F32),
            pltpu.VMEM((DGROUPS, SLOTS, LANES), F32),
            pltpu.VMEM((NT, SLOTS, LANES), F32),
            pltpu.VMEM((LANES, LANES), F32),
            pltpu.VMEM((2, NT, 8, LANES), F32),
            pltpu.VMEM((2, NT, 8, LANES), F32),
            pltpu.SemaphoreType.DMA((SLOTS + 4,)),
            pltpu.SemaphoreType.DMA((18,)),
            pltpu.SemaphoreType.DMA((18,)),
        ],
        compiler_params=pltpu.CompilerParams(
            collective_id=0, has_side_effects=True, vmem_limit_bytes=56000000
        ),
    )(
        counts,
        tile_rows.reshape(1, SLOTS),
        tile_cols.reshape(1, SLOTS),
        tiles.reshape(SLOTS, TILE, TILE),
        start_block,
    )
    return pl.pallas_call(
        hand_over,
        out_shape=shapes,
        in_specs=[vmem, vmem, vmem],
        out_specs=(vmem, vmem, vmem),
        compiler_params=pltpu.CompilerParams(vmem_limit_bytes=8 * 1024 * 1024),
    )(*results)


def solution(mesh):
    return jax.shard_map(
        on_device,
        mesh=mesh,
        in_specs=(
            P("doc", "term", None, None, None),
            P("doc", "term", None),
            P("doc", "term", None),
            P("doc", "term"),
            P(None, "term"),
        ),
        out_specs=(P(None, ("doc", "term")), P(None, ("term", "doc")), P()),
        check_vma=False,
    )
```

```python
import functools

import jax
import jax.numpy as jnp
from jax import lax
from jax.experimental import pallas as pl
from jax.experimental.pallas import tpu as pltpu
from jax.sharding import PartitionSpec as P

MESH = pl.DeviceIdType.MESH
F32 = jnp.float32
BF16 = jnp.bfloat16
TILE = 512
BLOCK = 16
SLOTS = 8
LANES = SLOTS * BLOCK
TERM_TILES = 64
DOC_TILES = 32
ND = 8
NT = 16
DX = TILE // ND
TX = TILE // NT
DGROUPS = DOC_TILES * BLOCK // LANES
TGROUPS = TERM_TILES * BLOCK // LANES
N_DOCS = ND * DOC_TILES * TILE
N_TERMS = NT * TERM_TILES * TILE
HIGHEST = lax.Precision.HIGHEST


def dot(a, b, contract, precision=HIGHEST):
    return lax.dot_general(
        a, b, (contract, ((), ())), precision=precision, preferred_element_type=F32
    )


NN = ((1,), (0,))
NTR = ((1,), (1,))
TN = ((0,), (0,))


def halves(x):
    hi = x.astype(BF16)
    lo = (x - hi.astype(F32)).astype(BF16)
    return jnp.concatenate([hi, lo], axis=0)


def iota(shape, dim):
    return lax.broadcasted_iota(jnp.int32, shape, dim)


def roll(x, shift):
    return pltpu.roll(x, shift, 1)


def fold(t):
    same = iota((LANES, LANES), 0) // BLOCK == iota((LANES, LANES), 1) // BLOCK
    t = jnp.where(same, t, 0.0)
    w = t[0:BLOCK]
    for g in range(1, SLOTS):
        w = w + t[g * BLOCK : (g + 1) * BLOCK]
    w = w + roll(w, 64)
    w = w + roll(w, 32)
    return w + roll(w, 16)


def packed(s, r):
    group = iota((8, LANES), 1) // BLOCK
    z = jnp.where(group == 0, s[0:8], s[8:16])
    if r is None:
        return z
    return jnp.where(group < 2, z, jnp.where(group == 2, r[0:8], r[8:16]))


def unpacked(z, first):
    lane = iota((BLOCK, LANES), 1)
    top = z if first == 0 else roll(z, LANES - BLOCK * first)
    low = roll(z, LANES - BLOCK * (first + 1))
    return jnp.where(lane < BLOCK, jnp.concatenate([top, low], axis=0), 0.0)


def spread(m):
    same = iota((LANES, LANES), 0) // BLOCK == iota((LANES, LANES), 1) // BLOCK
    r = m + roll(m, 16)
    r = r + roll(r, 32)
    r = r + roll(r, 64)
    return jnp.where(same, jnp.concatenate([r] * SLOTS, axis=0), 0.0)


def factor(s):
    lane = iota((BLOCK, LANES), 1)
    sub = iota((BLOCK, LANES), 0)
    m = jnp.where(lane < BLOCK, s, jnp.where(lane == sub + BLOCK, 1.0, 0.0))
    for c in range(BLOCK - 1):
        ratio = m[c : c + 1, :] / m[c : c + 1, c : c + 1]
        m = m - jnp.where(sub > c, m[:, c : c + 1], 0.0) * ratio
    diag = jnp.sum(jnp.where(lane == sub, m, 0.0), axis=1, keepdims=True)
    m = m * lax.rsqrt(diag)
    upper = jnp.where((lane < BLOCK) & (lane >= sub), m, 0.0)
    inverse = jnp.where(lane < BLOCK, roll(m, LANES - BLOCK), 0.0)
    return upper, inverse


def transposed(m):
    full = jnp.concatenate([m, jnp.zeros((LANES - BLOCK, LANES), F32)], axis=0)
    return full.T[:BLOCK, :]


def kernel(
    cnt_h, rows_h, cols_h, tiles_h, start_h,
    left_o, right_o, coef_o,
    cnt_s, rows_s, cols_s, tiles_v, start_v, st_v, sd_v,
    m1_v, d1_v, cs_v,
    tsend, trecv, dsend, drecv, za, zb,
    slots_v, share_v, cst_v, rs_v, rsr_v, rst_v, pk_v, pkr_v,
    load_sem, send_sem, recv_sem,
):
    i = lax.axis_index("doc")
    j = lax.axis_index("term")
    bar = pltpu.get_barrier_semaphore()
    for d in range(1, NT):
        pl.semaphore_signal(bar, 1, device_id=(i, lax.rem(j + d, NT)), device_id_type=MESH)
    for d in range(1, ND):
        pl.semaphore_signal(bar, 1, device_id=(lax.rem(i + d, ND), j), device_id_type=MESH)

    def load_start(t, carry):
        columns = pl.ds(pl.multiple_of(t * TILE, TILE), TILE)
        pltpu.make_async_copy(start_h.at[:, columns], start_v.at[t], load_sem.at[SLOTS]).start()
        return carry

    lax.fori_loop(0, TERM_TILES, load_start, 0)
    rows_load = pltpu.make_async_copy(rows_h, rows_s, load_sem.at[SLOTS + 1])
    cols_load = pltpu.make_async_copy(cols_h, cols_s, load_sem.at[SLOTS + 2])
    cnt_load = pltpu.make_async_copy(cnt_h, cnt_s, load_sem.at[SLOTS + 3])
    cnt_load.start()
    rows_load.start()
    cols_load.start()
    loads = []
    for k in range(SLOTS):
        load = pltpu.make_async_copy(tiles_h.at[k], tiles_v.at[k], load_sem.at[k])
        load.start()
        loads.append(load)

    pending = []

    def to_terms(n, src_of, dst):
        def send(d, carry):
            q = lax.rem(j + d, NT)
            pltpu.make_async_remote_copy(
                src_ref=src_of(q), dst_ref=dst.at[j],
                send_sem=send_sem.at[n], recv_sem=recv_sem.at[n, 0],
                device_id=(i, q), device_id_type=MESH,
            ).start()
            return carry
        lax.fori_loop(1, NT, send, 0)
        pending.append((n, dst.at[pl.ds(0, NT - 1)]))

    def to_docs(n, src_of, dst):
        def send(d, carry):
            q = lax.rem(i + d, ND)
            pltpu.make_async_remote_copy(
                src_ref=src_of(q), dst_ref=dst.at[i],
                send_sem=send_sem.at[n], recv_sem=recv_sem.at[n, 0],
                device_id=(q, j), device_id_type=MESH,
            ).start()
            return carry
        lax.fori_loop(1, ND, send, 0)
        pending.append((n, dst.at[pl.ds(0, ND - 1)]))

    def arrived(n, dst, peers, group=0):
        part = dst.at[pl.ds(0, peers - 1)]
        pltpu.make_async_copy(part, part, recv_sem.at[n, group]).wait()

    y = j // 4
    t0 = lax.rem(j, 4)
    xl = i // 4
    z0 = lax.rem(i, 4)

    def term_block_send(n, slot, block, dy):
        yb = lax.rem(y + dy, 4)
        tsend[slot, pl.ds(4 * yb, 4)] = block.reshape(4, TX, LANES)
        if dy == 0:
            trecv[slot, j] = tsend[slot, j]
            pending.append((n, trecv.at[slot, pl.ds(0, NT - 1)]))
        for t in (2, 3, 1) if dy == 0 else (2, 3, 1, 0):
            q = 4 * yb + lax.rem(t0 + t, 4)
            pltpu.make_async_remote_copy(
                src_ref=tsend.at[slot, q], dst_ref=trecv.at[slot, j],
                send_sem=send_sem.at[n], recv_sem=recv_sem.at[n, 1 if dy == 2 else 0],
                device_id=(i, q), device_id_type=MESH,
            ).start()

    def doc_block_send(n, slot, block, dx):
        xb = lax.rem(xl + dx, 2)
        dsend[slot, pl.ds(4 * xb, 4)] = block.reshape(4, DX, LANES)
        if dx == 0:
            drecv[slot, i] = dsend[slot, i]
            pending.append((n, drecv.at[slot, pl.ds(0, ND - 1)]))
        for t in (2, 1, 3) if dx == 0 else (2, 1, 3, 0):
            q = 4 * xb + lax.rem(z0 + t, 4)
            pltpu.make_async_remote_copy(
                src_ref=dsend.at[slot, q], dst_ref=drecv.at[slot, i],
                send_sem=send_sem.at[n], recv_sem=recv_sem.at[n, dx],
                device_id=(q, j), device_id_type=MESH,
            ).start()

    def forward_exchange(n, slot, x):
        lane_slot = iota((TILE, LANES), 1) // BLOCK
        weights = []
        for k in range(SLOTS):
            masked = [jnp.where(lane_slot == k, part, 0.0).astype(BF16) for part in x]
            weights.append(masked[0] if len(masked) == 1 else jnp.concatenate(masked, axis=1))
        for pair in ((2, 1), (3, 0)):
            rows = [pl.ds(pl.multiple_of(128 * lax.rem(y + dy, 4), 128), 128) for dy in pair]
            total = None
            for k in range(SLOTS):
                lhs = jnp.concatenate([tiles_v[k, r, :] for r in rows], axis=0)
                part = dot(lhs, weights[k], NN, None)
                total = part if total is None else total + part
            if len(x) == 2:
                total = total[:, :LANES] + total[:, LANES:]
            term_block_send(n, slot, total[:128], pair[0])
            term_block_send(n, slot, total[128:], pair[1])

    def term_sum(n, slot):
        acc = None
        for rel in (0, 1, 3, 2):
            if rel == 0:
                arrived(n, trecv.at[slot], 12)
            if rel == 2:
                arrived(n, trecv.at[slot], 5, 1)
            yb = lax.rem(y + rel, 4)
            block = trecv[slot, pl.ds(4 * yb, 4)]
            flat = jnp.concatenate([block[t] for t in range(4)], axis=1)
            onehot = st_v[:, pl.ds(pl.multiple_of(512 * yb, 512), 512)]
            part = dot(halves(flat), onehot, NTR, None)
            acc = part if acc is None else acc + part
        return acc[:TX] + acc[TX:]

    def term_gather(n, slot, x):
        both = halves(x)
        for dy in (2, 1, 3, 0):
            yb = lax.rem(y + dy, 4)
            part = dot(both, st_v[:, pl.ds(pl.multiple_of(512 * yb, 512), 512)], NN, None)
            term_block_send(n, slot, stacked(part[:TX] + part[TX:], 4), dy)

    def doc_sum(n, slot):
        acc = None
        for dx in (0, 1):
            arrived(n, drecv.at[slot], 4 + dx, dx)
            xb = lax.rem(xl + dx, 2)
            block = drecv[slot, pl.ds(4 * xb, 4)]
            flat = jnp.concatenate([block[t] for t in range(4)], axis=1)
            onehot = sd_v[:, pl.ds(pl.multiple_of(512 * xb, 512), 512)]
            part = dot(halves(flat), onehot, NTR, None)
            acc = part if acc is None else acc + part
        return acc[:DX] + acc[DX:]

    def doc_gather(n, slot, x):
        both = halves(x)
        for dx in (1, 0):
            xb = lax.rem(xl + dx, 2)
            part = dot(both, sd_v[:, pl.ds(pl.multiple_of(512 * xb, 512), 512)], NN, None)
            doc_block_send(n, slot, stacked(part[:DX] + part[DX:], 4), dx)

    def split(x):
        hi = x.astype(BF16).astype(F32)
        return [hi, x - hi]

    def stacked(x, groups):
        return jnp.concatenate([x[:, g * LANES : (g + 1) * LANES] for g in range(groups)], axis=0)

    def flat_of(x, groups):
        n = x.shape[0] // groups
        return jnp.concatenate([x[g * n : (g + 1) * n] for g in range(groups)], axis=1)

    def pack(x, out):
        group = iota((8, LANES), 1) // (2 * BLOCK)
        for g in range(DGROUPS):
            rows = [x[g * TX + 8 * h : g * TX + 8 * (h + 1)] for h in range(4)]
            for m in range(4):
                total = None
                for h in range(4):
                    shift = (32 * (h - m)) % LANES
                    turned = rows[h] if shift == 0 else roll(rows[h], shift)
                    total = turned if total is None else jnp.where(group == h, turned, total)
                out[4 * g + m] = total

    def unpack(ref):
        rows = []
        for q in range(NT):
            for h in range(4):
                rows.append(ref[q] if h == 0 else roll(ref[q], LANES - 32 * h))
        return jnp.concatenate(rows, axis=0)

    def all_sum(n, base, z):
        za[n, i] = z
        to_docs(base, lambda q: za.at[n, i], za.at[n])

        def rest():
            arrived(base, za.at[n], ND)
            s = za[n, 0]
            for q in range(1, ND):
                s = s + za[n, q]
            zb[n, j] = s
            to_terms(base + 1, lambda q: zb.at[n, j], zb.at[n])

        def last():
            arrived(base + 1, zb.at[n], NT)
            s = zb[n, 0]
            for q in range(1, NT):
                s = s + zb[n, q]
            return s

        return rest, last

    pltpu.make_async_copy(start_v, start_v, load_sem.at[SLOTS]).wait()
    acc = jnp.zeros((2 * LANES, 2 * LANES), F32)
    for ch in range(8):
        both = halves(start_v[ch * 8 : (ch + 1) * 8].reshape(LANES, TILE))
        acc = acc + dot(both, both, NTR, None)
    t = acc[:LANES, :LANES] + acc[:LANES, LANES:] + acc[LANES:, :LANES] + acc[LANES:, LANES:]
    start_gram = packed(fold(t) * (1.0 / N_TERMS), None)

    cnt_load.wait()
    rows_load.wait()
    cols_load.wait()
    lane8 = iota((8, LANES), 1)
    sub8 = iota((8, LANES), 0)
    cnt = cnt_s[0, 0]
    row_at = jnp.zeros((8, LANES), jnp.int32)
    my_col = jnp.zeros((8, LANES), jnp.int32)
    col_of = jnp.zeros((8, LANES), jnp.int32)
    row_of = jnp.zeros((8, LANES), jnp.int32)
    for k in range(SLOTS):
        here = lane8 // BLOCK == k
        row_at = jnp.where(here, rows_s[0, k] * BLOCK, row_at)
        my_col = jnp.where(here, cols_s[0, k], my_col)
        col_of = jnp.where(sub8 == k, cols_s[0, k], col_of)
        row_of = jnp.where(sub8 == k, rows_s[0, k], row_of)
    row_at = jnp.where(lane8 // BLOCK < cnt, row_at, -100000)
    my_col = jnp.where(lane8 // BLOCK < cnt, my_col, -10000)
    col_of = jnp.where(sub8 < cnt, col_of, -10000)
    row_of = jnp.where(sub8 < cnt, row_of, -10000)
    col_at = my_col * BLOCK
    row_at = (row_at + lane8 % BLOCK).astype(F32)
    col_at = (col_at + lane8 % BLOCK).astype(F32)
    my_col = my_col.astype(F32)
    d1_v[i] = jnp.concatenate([col_of.astype(F32), col_at], axis=0)
    m1_v[j] = jnp.concatenate([start_gram, row_at, row_of.astype(F32)], axis=0)

    col_sums = jnp.zeros((16, TILE), F32)
    for k in range(SLOTS):
        loads[k].wait()
        ones = jnp.where(iota((16, TILE), 0) == k, 1.0, 0.0).astype(BF16)
        col_sums = col_sums + dot(ones, tiles_v[k], NN, None)
    cs_v[i] = col_sums[:SLOTS]

    pl.semaphore_wait(bar, ND - 1 + NT - 1)
    to_docs(0, lambda q: d1_v.at[i], d1_v)
    to_docs(1, lambda q: cs_v.at[i], cs_v)
    to_terms(2, lambda q: m1_v.at[j], m1_v)

    row_sums = jnp.zeros((16, TILE), F32)
    for k in range(SLOTS):
        ones = jnp.where(iota((16, TILE), 0) == k, 1.0, 0.0).astype(BF16)
        row_sums = row_sums + dot(ones, tiles_v[k], NTR, None)
    for g in range(DGROUPS):
        rs_v[g] = row_sums[:SLOTS, g * LANES : (g + 1) * LANES]
    rsr_v[j] = rs_v[j // 4]
    to_terms(3, lambda q: rs_v.at[q // 4], rsr_v)
    slots_t = jnp.concatenate([start_v[cols_s[0, k]] for k in range(SLOTS)], axis=0).T
    slots_v[...] = slots_t

    arrived(0, d1_v, ND)
    arrived(1, cs_v, ND)
    cols_in = jnp.concatenate([d1_v[q, 0:8, :] for q in range(ND)], axis=0)
    sums_t = jnp.concatenate([cs_v[q] for q in range(ND)], axis=0).T
    cst_v[...] = sums_t
    same_col = jnp.where(cols_in == my_col[0:1, :], 1.0, 0.0)
    col_scale = lax.rsqrt(dot(sums_t, same_col, NN) + 1.0)
    scaled_slots = slots_v[...] * col_scale
    arrived(2, m1_v, NT)
    gram = m1_v[0, 0:8, :]
    for q in range(1, NT):
        gram = gram + m1_v[q, 0:8, :]
    _, inverse0 = factor(unpacked(gram, 0))
    k0 = spread(inverse0)
    forward_exchange(4, 1, [dot(scaled_slots, k0, NTR)])

    for q in range(NT):
        hit = iota((DOC_TILES * BLOCK, LANES), 0).astype(F32) == m1_v[q, 8:9, :]
        st_v[:, q * LANES : (q + 1) * LANES] = jnp.where(hit, 1.0, 0.0).astype(BF16)
    rows_in = jnp.concatenate([m1_v[q, 16:24, :] for q in range(NT)], axis=0)
    rows_wide = jnp.concatenate([rows_in] * DGROUPS, axis=1)
    row_tile = (iota((LANES, DOC_TILES * BLOCK), 1) // BLOCK).astype(F32)
    same_row = jnp.where(rows_wide == row_tile, 1.0, 0.0)
    arrived(3, rsr_v, NT)
    rst_v[...] = jnp.concatenate([rsr_v[q] for q in range(NT)], axis=0).T
    my_rows = rst_v[pl.ds(pl.multiple_of(TX * lax.rem(j, 4), TX), TX), :]
    row_scale = lax.rsqrt(dot(my_rows, same_row, NN) + 1.0)
    row_square = row_scale * row_scale

    image = term_sum(4, 1)
    term_gather(5, 2, image * row_square)
    f0 = stacked(image * row_scale, DGROUPS)
    rest, last = all_sum(0, 6, packed(fold(dot(f0, f0, TN)) * (1.0 / N_DOCS), None))
    pack(f0, pk_v.at[0])
    pkr_v[0, j] = pk_v[0, j]
    to_terms(8, lambda q: pk_v.at[0, q], pkr_v.at[0])

    for q in range(ND):
        hit = iota((TERM_TILES * BLOCK, LANES), 0).astype(F32) == d1_v[q, 8:9, :]
        sd_v[:, q * LANES : (q + 1) * LANES] = jnp.where(hit, 1.0, 0.0).astype(BF16)
    rest()
    arrived(5, trecv.at[2], 12)
    arrived(5, trecv.at[2], 5, 1)
    pieces = jnp.concatenate([trecv[2, q] for q in range(NT)], axis=0).T
    hi = pieces.astype(BF16)
    lo = (pieces - hi.astype(F32)).astype(BF16)
    pairs = []
    for k in range(SLOTS):
        part = slice(k * BLOCK, (k + 1) * BLOCK)
        pairs.append(jnp.concatenate([hi[part], lo[part]], axis=0))
    for dx in (1, 0):
        columns = pl.ds(pl.multiple_of(256 * lax.rem(xl + dx, 2), 256), 256)
        back = []
        for k in range(SLOTS):
            both = dot(pairs[k], tiles_v[k, :, columns], NN, None)
            back.append(both[:BLOCK] + both[BLOCK:])
        doc_block_send(9, 0, jnp.concatenate(back, axis=0).T, dx)

    cols_wide = jnp.concatenate([cols_in] * TGROUPS, axis=1)
    tile_at = (iota((ND * SLOTS, TERM_TILES * BLOCK), 1) // BLOCK).astype(F32)
    my_sums = cst_v[pl.ds(pl.multiple_of(i * DX, DX), DX), :]
    col_share = lax.rsqrt(dot(my_sums, jnp.where(cols_wide == tile_at, 1.0, 0.0), NN) + 1.0)
    col_square = col_share * col_share
    window = pl.ds(pl.multiple_of(128 * (i // 2), 128), 128)
    for g in range(TGROUPS):
        share_v[g] = start_v[g * 8 : (g + 1) * 8, :, window].reshape(LANES, 128).T
    half = pl.multiple_of(DX * lax.rem(i, 2), DX)
    start_share = jnp.concatenate([share_v[g, pl.ds(half, DX), :] for g in range(TGROUPS)], axis=0)
    e_share = dot(start_share, k0, NTR)
    upper1, inverse1 = factor(unpacked(last(), 0))
    k1 = spread(inverse1)
    p0 = upper1 * (N_DOCS / N_TERMS)
    expected = dot(e_share, spread(p0), NTR)
    u1 = dot(f0, k1, NTR)

    image = doc_sum(9, 0)
    doc_gather(10, 1, image * col_square)
    b1 = dot(stacked(image * col_share, TGROUPS), k1, NTR) - expected
    t2 = dot(b1, jnp.concatenate([b1, e_share], axis=1), TN) * (1.0 / N_TERMS)
    rest, last = all_sum(1, 11, packed(fold(t2[:, :LANES]), fold(t2[:, LANES:])))
    for g in range(TGROUPS):
        share_v[g, 0:DX, :] = b1[g * DX : (g + 1) * DX]
    drecv[2, i] = share_v[i, 0:DX, :]
    to_docs(13, lambda q: share_v.at[q, pl.ds(0, DX), :], drecv.at[2])

    rest()
    arrived(10, drecv.at[1], 4)
    arrived(10, drecv.at[1], 5, 1)
    pieces = jnp.concatenate([drecv[1, q] for q in range(ND)], axis=0)
    forward_exchange(14, 3, split(pieces))
    z = last()
    r1 = unpacked(z, 2)
    pad = jnp.zeros((LANES - BLOCK, LANES), F32)
    g2 = unpacked(z, 0) - dot(r1, jnp.concatenate([r1, pad], axis=0), NTR)
    upper2, inverse2 = factor(g2)
    k2 = spread(inverse2)
    kr1 = spread(r1)
    p02 = upper2 * (N_TERMS / N_DOCS)
    k21 = dot(k2, k1, NN)
    known = dot(k2, spread(p0 + r1), NN) + dot(spread(p02), k1, NN)
    expected = dot(f0, known, NTR)

    image = term_sum(14, 3) * row_scale
    x2 = dot(stacked(image, DGROUPS), k21, NTR) - expected
    t3 = dot(x2, jnp.concatenate([x2, u1], axis=1), TN) * (1.0 / N_DOCS)
    rest, last = all_sum(2, 15, packed(fold(t3[:, :LANES]), fold(t3[:, LANES:])))
    pack(x2, pk_v.at[1])
    pkr_v[1, j] = pk_v[1, j]
    to_terms(17, lambda q: pk_v.at[1, q], pkr_v.at[1])
    arrived(13, drecv.at[2], ND)
    right_x = jnp.concatenate([drecv[2, q] for q in range(ND)], axis=0)
    rest()

    start_st = start_v[pl.ds(i * 8, 8)].reshape(LANES, TILE)
    k20 = dot(k2, dot(kr1, k0, NN), NN)
    right = dot(k2, right_x, NTR) - dot(k20, start_st, NN)
    for g in range(8):
        right_o[:, g * TILE : (g + 1) * TILE] = right[g * BLOCK : (g + 1) * BLOCK]
    coef_o[0] = transposed(upper1)[:, :BLOCK]
    coef_o[1] = (p0 + r1)[:, :BLOCK]
    coef_o[2] = transposed(upper2)[:, :BLOCK]
    arrived(8, pkr_v.at[0], NT)
    left_u = dot(unpack(pkr_v.at[0]), k1, NTR)
    arrived(17, pkr_v.at[1], NT)
    left_x = unpack(pkr_v.at[1])

    z = last()
    r2 = unpacked(z, 2)
    g3 = unpacked(z, 0) - dot(r2, jnp.concatenate([r2, pad], axis=0), NTR)
    upper3, inverse3 = factor(g3)
    left_x = left_x - dot(left_u, spread(r2), NTR)
    rep = inverse3 + roll(inverse3, 16)
    rep = rep + roll(rep, 32)
    rep = rep + roll(rep, 64)
    mine = iota((2 * BLOCK, LANES), 1) // BLOCK == iota((2 * BLOCK, LANES), 0) // BLOCK
    left = dot(jnp.where(mine, jnp.concatenate([rep, rep], axis=0), 0.0), left_x, NTR)
    left_o[:, 0:TILE] = left[0:BLOCK]
    left_o[:, TILE : 2 * TILE] = left[BLOCK : 2 * BLOCK]
    coef_o[3] = (p02 + r2)[:, :BLOCK]
    coef_o[4] = transposed(upper3)[:, :BLOCK]
    for n, part in pending:
        pltpu.make_async_copy(part, part, send_sem.at[n]).wait()


def hand_over(left_i, right_i, coef_i, left_o, right_o, coef_o):
    left_o[...] = left_i[...]
    right_o[...] = right_i[...]
    coef_o[...] = coef_i[...]


def on_device(tiles, tile_rows, tile_cols, counts, start_block):
    anywhere = pl.BlockSpec(memory_space=pl.ANY)
    vmem = pl.BlockSpec(memory_space=pltpu.VMEM)
    shapes = (
        jax.ShapeDtypeStruct((BLOCK, DOC_TILES * TILE // NT), F32),
        jax.ShapeDtypeStruct((BLOCK, TERM_TILES * TILE // ND), F32),
        jax.ShapeDtypeStruct((5, BLOCK, BLOCK), F32),
    )
    results = pl.pallas_call(
        kernel,
        out_shape=shapes,
        in_specs=[anywhere] * 5,
        out_specs=(vmem, vmem, vmem),
        scratch_shapes=[
            pltpu.SMEM((1, 1), jnp.int32),
            pltpu.SMEM((1, SLOTS), jnp.int32),
            pltpu.SMEM((1, SLOTS), jnp.int32),
            pltpu.VMEM((SLOTS, TILE, TILE), BF16),
            pltpu.VMEM((TERM_TILES, BLOCK, TILE), F32),
            pltpu.VMEM((DOC_TILES * BLOCK, NT * LANES), BF16),
            pltpu.VMEM((TERM_TILES * BLOCK, ND * LANES), BF16),
            pltpu.VMEM((NT, 24, LANES), F32),
            pltpu.VMEM((ND, 16, LANES), F32),
            pltpu.VMEM((ND, SLOTS, TILE), F32),
            pltpu.VMEM((4, NT, TX, LANES), F32),
            pltpu.VMEM((4, NT, TX, LANES), F32),
            pltpu.VMEM((2, ND, DX, LANES), F32),
            pltpu.VMEM((3, ND, DX, LANES), F32),
            pltpu.VMEM((3, ND, 8, LANES), F32),
            pltpu.VMEM((3, NT, 8, LANES), F32),
            pltpu.VMEM((TILE, LANES), F32),
            pltpu.VMEM((TGROUPS, LANES, LANES), F32),
            pltpu.VMEM((TILE, ND * SLOTS), F32),
            pltpu.VMEM((DGROUPS, SLOTS, LANES), F32),
            pltpu.VMEM((NT, SLOTS, LANES), F32),
            pltpu.VMEM((LANES, LANES), F32),
            pltpu.VMEM((2, NT, 8, LANES), F32),
            pltpu.VMEM((2, NT, 8, LANES), F32),
            pltpu.SemaphoreType.DMA((SLOTS + 4,)),
            pltpu.SemaphoreType.DMA((18,)),
            pltpu.SemaphoreType.DMA((18, 2)),
        ],
        compiler_params=pltpu.CompilerParams(
            collective_id=0, has_side_effects=True, vmem_limit_bytes=56000000
        ),
    )(
        counts,
        tile_rows.reshape(1, SLOTS),
        tile_cols.reshape(1, SLOTS),
        tiles.reshape(SLOTS, TILE, TILE),
        start_block,
    )
    return pl.pallas_call(
        hand_over,
        out_shape=shapes,
        in_specs=[vmem, vmem, vmem],
        out_specs=(vmem, vmem, vmem),
        compiler_params=pltpu.CompilerParams(vmem_limit_bytes=8 * 1024 * 1024),
    )(*results)


def solution(mesh):
    return jax.shard_map(
        on_device,
        mesh=mesh,
        in_specs=(
            P("doc", "term", None, None, None),
            P("doc", "term", None),
            P("doc", "term", None),
            P("doc", "term"),
            P(None, "term"),
        ),
        out_specs=(P(None, ("doc", "term")), P(None, ("term", "doc")), P()),
        check_vma=False,
    )
```

```python
import functools

import jax
import jax.numpy as jnp
from jax import lax
from jax.experimental import pallas as pl
from jax.experimental.pallas import tpu as pltpu
from jax.sharding import PartitionSpec as P

MESH = pl.DeviceIdType.MESH
F32 = jnp.float32
BF16 = jnp.bfloat16
TILE = 512
BLOCK = 16
SLOTS = 8
LANES = SLOTS * BLOCK
TERM_TILES = 64
DOC_TILES = 32
ND = 8
NT = 16
DX = TILE // ND
TX = TILE // NT
DGROUPS = DOC_TILES * BLOCK // LANES
TGROUPS = TERM_TILES * BLOCK // LANES
N_DOCS = ND * DOC_TILES * TILE
N_TERMS = NT * TERM_TILES * TILE
HIGHEST = lax.Precision.HIGHEST


def dot(a, b, contract, precision=HIGHEST):
    return lax.dot_general(
        a, b, (contract, ((), ())), precision=precision, preferred_element_type=F32
    )


NN = ((1,), (0,))
NTR = ((1,), (1,))
TN = ((0,), (0,))


def halves(x):
    hi = x.astype(BF16)
    lo = (x - hi.astype(F32)).astype(BF16)
    return jnp.concatenate([hi, lo], axis=0)


def iota(shape, dim):
    return lax.broadcasted_iota(jnp.int32, shape, dim)


def roll(x, shift):
    return pltpu.roll(x, shift, 1)


def fold(t):
    same = iota((LANES, LANES), 0) // BLOCK == iota((LANES, LANES), 1) // BLOCK
    t = jnp.where(same, t, 0.0)
    w = t[0:BLOCK]
    for g in range(1, SLOTS):
        w = w + t[g * BLOCK : (g + 1) * BLOCK]
    w = w + roll(w, 64)
    w = w + roll(w, 32)
    return w + roll(w, 16)


def packed(s, r):
    group = iota((8, LANES), 1) // BLOCK
    z = jnp.where(group == 0, s[0:8], s[8:16])
    if r is None:
        return z
    return jnp.where(group < 2, z, jnp.where(group == 2, r[0:8], r[8:16]))


def unpacked(z, first):
    lane = iota((BLOCK, LANES), 1)
    top = z if first == 0 else roll(z, LANES - BLOCK * first)
    low = roll(z, LANES - BLOCK * (first + 1))
    return jnp.where(lane < BLOCK, jnp.concatenate([top, low], axis=0), 0.0)


def spread(m):
    same = iota((LANES, LANES), 0) // BLOCK == iota((LANES, LANES), 1) // BLOCK
    r = m + roll(m, 16)
    r = r + roll(r, 32)
    r = r + roll(r, 64)
    return jnp.where(same, jnp.concatenate([r] * SLOTS, axis=0), 0.0)


def factor(s):
    lane = iota((BLOCK, LANES), 1)
    sub = iota((BLOCK, LANES), 0)
    m = jnp.where(lane < BLOCK, s, jnp.where(lane == sub + BLOCK, 1.0, 0.0))
    for c in range(BLOCK - 1):
        ratio = m[c : c + 1, :] / m[c : c + 1, c : c + 1]
        m = m - jnp.where(sub > c, m[:, c : c + 1], 0.0) * ratio
    diag = jnp.sum(jnp.where(lane == sub, m, 0.0), axis=1, keepdims=True)
    m = m * lax.rsqrt(diag)
    upper = jnp.where((lane < BLOCK) & (lane >= sub), m, 0.0)
    inverse = jnp.where(lane < BLOCK, roll(m, LANES - BLOCK), 0.0)
    return upper, inverse


def transposed(m):
    full = jnp.concatenate([m, jnp.zeros((LANES - BLOCK, LANES), F32)], axis=0)
    return full.T[:BLOCK, :]


def kernel(
    cnt_h, rows_h, cols_h, tiles_h, start_h,
    left_o, right_o, coef_o,
    cnt_s, rows_s, cols_s, tiles_v, start_v, st_v, sd_v,
    m1_v, d1_v, cs_v,
    tsend, trecv, dsend, drecv, za, zb,
    slots_v, share_v, cst_v, rs_v, rsr_v, rst_v, pk_v, pkr_v,
    load_sem, send_sem, recv_sem,
):
    i = lax.axis_index("doc")
    j = lax.axis_index("term")
    bar = pltpu.get_barrier_semaphore()
    for d in range(1, NT):
        pl.semaphore_signal(bar, 1, device_id=(i, lax.rem(j + d, NT)), device_id_type=MESH)
    for d in range(1, ND):
        pl.semaphore_signal(bar, 1, device_id=(lax.rem(i + d, ND), j), device_id_type=MESH)

    def load_start(t, carry):
        columns = pl.ds(pl.multiple_of(t * TILE, TILE), TILE)
        pltpu.make_async_copy(start_h.at[:, columns], start_v.at[t], load_sem.at[SLOTS]).start()
        return carry

    lax.fori_loop(0, TERM_TILES, load_start, 0)
    rows_load = pltpu.make_async_copy(rows_h, rows_s, load_sem.at[SLOTS + 1])
    cols_load = pltpu.make_async_copy(cols_h, cols_s, load_sem.at[SLOTS + 2])
    cnt_load = pltpu.make_async_copy(cnt_h, cnt_s, load_sem.at[SLOTS + 3])
    cnt_load.start()
    rows_load.start()
    cols_load.start()
    loads = []
    for k in range(SLOTS):
        load = pltpu.make_async_copy(tiles_h.at[k], tiles_v.at[k], load_sem.at[k])
        load.start()
        loads.append(load)

    pending = []

    def to_terms(n, src_of, dst):
        def send(d, carry):
            q = lax.rem(j + d, NT)
            pltpu.make_async_remote_copy(
                src_ref=src_of(q), dst_ref=dst.at[j],
                send_sem=send_sem.at[n], recv_sem=recv_sem.at[n, 0],
                device_id=(i, q), device_id_type=MESH,
            ).start()
            return carry
        lax.fori_loop(1, NT, send, 0)
        pending.append((n, dst.at[pl.ds(0, NT - 1)]))

    def to_docs(n, src_of, dst):
        def send(d, carry):
            q = lax.rem(i + d, ND)
            pltpu.make_async_remote_copy(
                src_ref=src_of(q), dst_ref=dst.at[i],
                send_sem=send_sem.at[n], recv_sem=recv_sem.at[n, 0],
                device_id=(q, j), device_id_type=MESH,
            ).start()
            return carry
        lax.fori_loop(1, ND, send, 0)
        pending.append((n, dst.at[pl.ds(0, ND - 1)]))

    def arrived(n, dst, peers, group=0):
        part = dst.at[pl.ds(0, peers - 1)]
        pltpu.make_async_copy(part, part, recv_sem.at[n, group]).wait()

    y = j // 4
    t0 = lax.rem(j, 4)
    xl = i // 4
    z0 = lax.rem(i, 4)

    def term_block_send(n, slot, block, dy, looped=False):
        yb = lax.rem(y + dy, 4)
        tsend[slot, pl.ds(4 * yb, 4)] = block.reshape(4, TX, LANES)
        if dy == 0:
            trecv[slot, j] = tsend[slot, j]
            pending.append((n, trecv.at[slot, pl.ds(0, NT - 1)]))

        def send(t, carry=0):
            q = 4 * yb + lax.rem(t0 + t, 4)
            pltpu.make_async_remote_copy(
                src_ref=tsend.at[slot, q], dst_ref=trecv.at[slot, j],
                send_sem=send_sem.at[n], recv_sem=recv_sem.at[n, 1 if dy == 2 else 0],
                device_id=(i, q), device_id_type=MESH,
            ).start()
            return carry

        if looped:
            lax.fori_loop(1, 4 if dy == 0 else 5, send, 0)
        else:
            for t in (2, 3, 1) if dy == 0 else (2, 3, 1, 0):
                send(t)

    def doc_block_send(n, slot, block, dx, looped=False):
        xb = lax.rem(xl + dx, 2)
        dsend[slot, pl.ds(4 * xb, 4)] = block.reshape(4, DX, LANES)
        if dx == 0:
            drecv[slot, i] = dsend[slot, i]
            pending.append((n, drecv.at[slot, pl.ds(0, ND - 1)]))

        def send(t, carry=0):
            q = 4 * xb + lax.rem(z0 + t, 4)
            pltpu.make_async_remote_copy(
                src_ref=dsend.at[slot, q], dst_ref=drecv.at[slot, i],
                send_sem=send_sem.at[n], recv_sem=recv_sem.at[n, dx],
                device_id=(q, j), device_id_type=MESH,
            ).start()
            return carry

        if looped:
            lax.fori_loop(1, 4 if dx == 0 else 5, send, 0)
        else:
            for t in (2, 1, 3) if dx == 0 else (2, 1, 3, 0):
                send(t)

    def forward_exchange(n, slot, x):
        lane_slot = iota((TILE, LANES), 1) // BLOCK
        weights = []
        for k in range(SLOTS):
            masked = [jnp.where(lane_slot == k, part, 0.0).astype(BF16) for part in x]
            weights.append(masked[0] if len(masked) == 1 else jnp.concatenate(masked, axis=1))
        for pair in ((2, 1), (3, 0)):
            rows = [pl.ds(pl.multiple_of(128 * lax.rem(y + dy, 4), 128), 128) for dy in pair]
            total = None
            for k in range(SLOTS):
                lhs = jnp.concatenate([tiles_v[k, r, :] for r in rows], axis=0)
                part = dot(lhs, weights[k], NN, None)
                total = part if total is None else total + part
            if len(x) == 2:
                total = total[:, :LANES] + total[:, LANES:]
            term_block_send(n, slot, total[:128], pair[0])
            term_block_send(n, slot, total[128:], pair[1])

    def term_sum(n, slot):
        acc = None
        for rel in (0, 1, 3, 2):
            if rel == 0:
                arrived(n, trecv.at[slot], 12)
            if rel == 2:
                arrived(n, trecv.at[slot], 5, 1)
            yb = lax.rem(y + rel, 4)
            block = trecv[slot, pl.ds(4 * yb, 4)]
            flat = jnp.concatenate([block[t] for t in range(4)], axis=1)
            onehot = st_v[:, pl.ds(pl.multiple_of(512 * yb, 512), 512)]
            part = dot(halves(flat), onehot, NTR, None)
            acc = part if acc is None else acc + part
        return acc[:TX] + acc[TX:]

    def term_gather(n, slot, x):
        both = halves(x)
        for dy in (2, 1, 3, 0):
            yb = lax.rem(y + dy, 4)
            part = dot(both, st_v[:, pl.ds(pl.multiple_of(512 * yb, 512), 512)], NN, None)
            term_block_send(n, slot, stacked(part[:TX] + part[TX:], 4), dy, dy in (0, 2))

    def doc_sum(n, slot):
        acc = None
        for dx in (0, 1):
            arrived(n, drecv.at[slot], 4 + dx, dx)
            xb = lax.rem(xl + dx, 2)
            block = drecv[slot, pl.ds(4 * xb, 4)]
            flat = jnp.concatenate([block[t] for t in range(4)], axis=1)
            onehot = sd_v[:, pl.ds(pl.multiple_of(512 * xb, 512), 512)]
            part = dot(halves(flat), onehot, NTR, None)
            acc = part if acc is None else acc + part
        return acc[:DX] + acc[DX:]

    def doc_gather(n, slot, x):
        both = halves(x)
        for dx in (1, 0):
            xb = lax.rem(xl + dx, 2)
            part = dot(both, sd_v[:, pl.ds(pl.multiple_of(512 * xb, 512), 512)], NN, None)
            doc_block_send(n, slot, stacked(part[:DX] + part[DX:], 4), dx, True)

    def split(x):
        hi = x.astype(BF16).astype(F32)
        return [hi, x - hi]

    def stacked(x, groups):
        return jnp.concatenate([x[:, g * LANES : (g + 1) * LANES] for g in range(groups)], axis=0)

    def flat_of(x, groups):
        n = x.shape[0] // groups
        return jnp.concatenate([x[g * n : (g + 1) * n] for g in range(groups)], axis=1)

    def pack(x, out):
        group = iota((8, LANES), 1) // (2 * BLOCK)
        for g in range(DGROUPS):
            rows = [x[g * TX + 8 * h : g * TX + 8 * (h + 1)] for h in range(4)]
            for m in range(4):
                total = None
                for h in range(4):
                    shift = (32 * (h - m)) % LANES
                    turned = rows[h] if shift == 0 else roll(rows[h], shift)
                    total = turned if total is None else jnp.where(group == h, turned, total)
                out[4 * g + m] = total

    def unpack(ref):
        rows = []
        for q in range(NT):
            for h in range(4):
                rows.append(ref[q] if h == 0 else roll(ref[q], LANES - 32 * h))
        return jnp.concatenate(rows, axis=0)

    def all_sum(n, base, z):
        za[n, i] = z
        to_docs(base, lambda q: za.at[n, i], za.at[n])

        def rest():
            arrived(base, za.at[n], ND)
            s = za[n, 0]
            for q in range(1, ND):
                s = s + za[n, q]
            zb[n, j] = s
            to_terms(base + 1, lambda q: zb.at[n, j], zb.at[n])

        def last():
            arrived(base + 1, zb.at[n], NT)
            s = zb[n, 0]
            for q in range(1, NT):
                s = s + zb[n, q]
            return s

        return rest, last

    pltpu.make_async_copy(start_v, start_v, load_sem.at[SLOTS]).wait()
    acc = jnp.zeros((2 * LANES, 2 * LANES), F32)
    for ch in range(8):
        both = halves(start_v[ch * 8 : (ch + 1) * 8].reshape(LANES, TILE))
        acc = acc + dot(both, both, NTR, None)
    t = acc[:LANES, :LANES] + acc[:LANES, LANES:] + acc[LANES:, :LANES] + acc[LANES:, LANES:]
    start_gram = packed(fold(t) * (1.0 / N_TERMS), None)

    cnt_load.wait()
    rows_load.wait()
    cols_load.wait()
    lane8 = iota((8, LANES), 1)
    sub8 = iota((8, LANES), 0)
    cnt = cnt_s[0, 0]
    row_at = jnp.zeros((8, LANES), jnp.int32)
    my_col = jnp.zeros((8, LANES), jnp.int32)
    col_of = jnp.zeros((8, LANES), jnp.int32)
    row_of = jnp.zeros((8, LANES), jnp.int32)
    for k in range(SLOTS):
        here = lane8 // BLOCK == k
        row_at = jnp.where(here, rows_s[0, k] * BLOCK, row_at)
        my_col = jnp.where(here, cols_s[0, k], my_col)
        col_of = jnp.where(sub8 == k, cols_s[0, k], col_of)
        row_of = jnp.where(sub8 == k, rows_s[0, k], row_of)
    row_at = jnp.where(lane8 // BLOCK < cnt, row_at, -100000)
    my_col = jnp.where(lane8 // BLOCK < cnt, my_col, -10000)
    col_of = jnp.where(sub8 < cnt, col_of, -10000)
    row_of = jnp.where(sub8 < cnt, row_of, -10000)
    col_at = my_col * BLOCK
    row_at = (row_at + lane8 % BLOCK).astype(F32)
    col_at = (col_at + lane8 % BLOCK).astype(F32)
    my_col = my_col.astype(F32)
    d1_v[i] = jnp.concatenate([col_of.astype(F32), col_at], axis=0)
    m1_v[j] = jnp.concatenate([start_gram, row_at, row_of.astype(F32)], axis=0)

    col_sums = jnp.zeros((16, TILE), F32)
    for k in range(SLOTS):
        loads[k].wait()
        ones = jnp.where(iota((16, TILE), 0) == k, 1.0, 0.0).astype(BF16)
        col_sums = col_sums + dot(ones, tiles_v[k], NN, None)
    cs_v[i] = col_sums[:SLOTS]

    pl.semaphore_wait(bar, ND - 1 + NT - 1)
    to_docs(0, lambda q: d1_v.at[i], d1_v)
    to_docs(1, lambda q: cs_v.at[i], cs_v)
    to_terms(2, lambda q: m1_v.at[j], m1_v)

    row_sums = jnp.zeros((16, TILE), F32)
    for k in range(SLOTS):
        ones = jnp.where(iota((16, TILE), 0) == k, 1.0, 0.0).astype(BF16)
        row_sums = row_sums + dot(ones, tiles_v[k], NTR, None)
    for g in range(DGROUPS):
        rs_v[g] = row_sums[:SLOTS, g * LANES : (g + 1) * LANES]
    rsr_v[j] = rs_v[j // 4]
    to_terms(3, lambda q: rs_v.at[q // 4], rsr_v)
    slots_t = jnp.concatenate([start_v[cols_s[0, k]] for k in range(SLOTS)], axis=0).T
    slots_v[...] = slots_t

    arrived(0, d1_v, ND)
    arrived(1, cs_v, ND)
    cols_in = jnp.concatenate([d1_v[q, 0:8, :] for q in range(ND)], axis=0)
    sums_t = jnp.concatenate([cs_v[q] for q in range(ND)], axis=0).T
    cst_v[...] = sums_t
    same_col = jnp.where(cols_in == my_col[0:1, :], 1.0, 0.0)
    col_scale = lax.rsqrt(dot(sums_t, same_col, NN) + 1.0)
    scaled_slots = slots_v[...] * col_scale
    arrived(2, m1_v, NT)
    gram = m1_v[0, 0:8, :]
    for q in range(1, NT):
        gram = gram + m1_v[q, 0:8, :]
    _, inverse0 = factor(unpacked(gram, 0))
    k0 = spread(inverse0)
    forward_exchange(4, 1, [dot(scaled_slots, k0, NTR)])

    for q in range(NT):
        hit = iota((DOC_TILES * BLOCK, LANES), 0).astype(F32) == m1_v[q, 8:9, :]
        st_v[:, q * LANES : (q + 1) * LANES] = jnp.where(hit, 1.0, 0.0).astype(BF16)
    rows_in = jnp.concatenate([m1_v[q, 16:24, :] for q in range(NT)], axis=0)
    rows_wide = jnp.concatenate([rows_in] * DGROUPS, axis=1)
    row_tile = (iota((LANES, DOC_TILES * BLOCK), 1) // BLOCK).astype(F32)
    same_row = jnp.where(rows_wide == row_tile, 1.0, 0.0)
    arrived(3, rsr_v, NT)
    rst_v[...] = jnp.concatenate([rsr_v[q] for q in range(NT)], axis=0).T
    my_rows = rst_v[pl.ds(pl.multiple_of(TX * lax.rem(j, 4), TX), TX), :]
    row_scale = lax.rsqrt(dot(my_rows, same_row, NN) + 1.0)
    row_square = row_scale * row_scale

    image = term_sum(4, 1)
    term_gather(5, 2, image * row_square)
    f0 = stacked(image * row_scale, DGROUPS)
    rest, last = all_sum(0, 6, packed(fold(dot(f0, f0, TN)) * (1.0 / N_DOCS), None))
    pack(f0, pk_v.at[0])
    pkr_v[0, j] = pk_v[0, j]
    to_terms(8, lambda q: pk_v.at[0, q], pkr_v.at[0])

    for q in range(ND):
        hit = iota((TERM_TILES * BLOCK, LANES), 0).astype(F32) == d1_v[q, 8:9, :]
        sd_v[:, q * LANES : (q + 1) * LANES] = jnp.where(hit, 1.0, 0.0).astype(BF16)
    rest()
    arrived(5, trecv.at[2], 12)
    arrived(5, trecv.at[2], 5, 1)
    pieces = jnp.concatenate([trecv[2, q] for q in range(NT)], axis=0).T
    hi = pieces.astype(BF16)
    lo = (pieces - hi.astype(F32)).astype(BF16)
    pairs = []
    for k in range(SLOTS):
        part = slice(k * BLOCK, (k + 1) * BLOCK)
        pairs.append(jnp.concatenate([hi[part], lo[part]], axis=0))
    for dx in (1, 0):
        columns = pl.ds(pl.multiple_of(256 * lax.rem(xl + dx, 2), 256), 256)
        back = []
        for k in range(SLOTS):
            both = dot(pairs[k], tiles_v[k, :, columns], NN, None)
            back.append(both[:BLOCK] + both[BLOCK:])
        doc_block_send(9, 0, jnp.concatenate(back, axis=0).T, dx)

    cols_wide = jnp.concatenate([cols_in] * TGROUPS, axis=1)
    tile_at = (iota((ND * SLOTS, TERM_TILES * BLOCK), 1) // BLOCK).astype(F32)
    my_sums = cst_v[pl.ds(pl.multiple_of(i * DX, DX), DX), :]
    col_share = lax.rsqrt(dot(my_sums, jnp.where(cols_wide == tile_at, 1.0, 0.0), NN) + 1.0)
    col_square = col_share * col_share
    window = pl.ds(pl.multiple_of(128 * (i // 2), 128), 128)
    for g in range(TGROUPS):
        share_v[g] = start_v[g * 8 : (g + 1) * 8, :, window].reshape(LANES, 128).T
    half = pl.multiple_of(DX * lax.rem(i, 2), DX)
    start_share = jnp.concatenate([share_v[g, pl.ds(half, DX), :] for g in range(TGROUPS)], axis=0)
    e_share = dot(start_share, k0, NTR)
    upper1, inverse1 = factor(unpacked(last(), 0))
    k1 = spread(inverse1)
    p0 = upper1 * (N_DOCS / N_TERMS)
    expected = dot(e_share, spread(p0), NTR)
    u1 = dot(f0, k1, NTR)

    image = doc_sum(9, 0)
    doc_gather(10, 1, image * col_square)
    b1 = dot(stacked(image * col_share, TGROUPS), k1, NTR) - expected
    t2 = dot(b1, jnp.concatenate([b1, e_share], axis=1), TN) * (1.0 / N_TERMS)
    rest, last = all_sum(1, 11, packed(fold(t2[:, :LANES]), fold(t2[:, LANES:])))
    for g in range(TGROUPS):
        share_v[g, 0:DX, :] = b1[g * DX : (g + 1) * DX]
    drecv[2, i] = share_v[i, 0:DX, :]

    rest()
    arrived(10, drecv.at[1], 4)
    arrived(10, drecv.at[1], 5, 1)
    pieces = jnp.concatenate([drecv[1, q] for q in range(ND)], axis=0)
    forward_exchange(14, 3, split(pieces))
    to_docs(13, lambda q: share_v.at[q, pl.ds(0, DX), :], drecv.at[2])
    z = last()
    r1 = unpacked(z, 2)
    pad = jnp.zeros((LANES - BLOCK, LANES), F32)
    g2 = unpacked(z, 0) - dot(r1, jnp.concatenate([r1, pad], axis=0), NTR)
    upper2, inverse2 = factor(g2)
    k2 = spread(inverse2)
    kr1 = spread(r1)
    p02 = upper2 * (N_TERMS / N_DOCS)
    k21 = dot(k2, k1, NN)
    known = dot(k2, spread(p0 + r1), NN) + dot(spread(p02), k1, NN)
    expected = dot(f0, known, NTR)

    image = term_sum(14, 3) * row_scale
    x2 = dot(stacked(image, DGROUPS), k21, NTR) - expected
    t3 = dot(x2, jnp.concatenate([x2, u1], axis=1), TN) * (1.0 / N_DOCS)
    rest, last = all_sum(2, 15, packed(fold(t3[:, :LANES]), fold(t3[:, LANES:])))
    pack(x2, pk_v.at[1])
    pkr_v[1, j] = pk_v[1, j]
    to_terms(17, lambda q: pk_v.at[1, q], pkr_v.at[1])
    rest()
    arrived(13, drecv.at[2], ND)
    right_x = jnp.concatenate([drecv[2, q] for q in range(ND)], axis=0)

    start_st = start_v[pl.ds(i * 8, 8)].reshape(LANES, TILE)
    k20 = dot(k2, dot(kr1, k0, NN), NN)
    right = dot(k2, right_x, NTR) - dot(k20, start_st, NN)
    for g in range(8):
        right_o[:, g * TILE : (g + 1) * TILE] = right[g * BLOCK : (g + 1) * BLOCK]
    coef_o[0] = transposed(upper1)[:, :BLOCK]
    coef_o[1] = (p0 + r1)[:, :BLOCK]
    coef_o[2] = transposed(upper2)[:, :BLOCK]
    arrived(8, pkr_v.at[0], NT)
    left_u = dot(unpack(pkr_v.at[0]), k1, NTR)
    arrived(17, pkr_v.at[1], NT)
    left_x = unpack(pkr_v.at[1])

    z = last()
    r2 = unpacked(z, 2)
    g3 = unpacked(z, 0) - dot(r2, jnp.concatenate([r2, pad], axis=0), NTR)
    upper3, inverse3 = factor(g3)
    left_x = left_x - dot(left_u, spread(r2), NTR)
    rep = inverse3 + roll(inverse3, 16)
    rep = rep + roll(rep, 32)
    rep = rep + roll(rep, 64)
    mine = iota((2 * BLOCK, LANES), 1) // BLOCK == iota((2 * BLOCK, LANES), 0) // BLOCK
    left = dot(jnp.where(mine, jnp.concatenate([rep, rep], axis=0), 0.0), left_x, NTR)
    left_o[:, 0:TILE] = left[0:BLOCK]
    left_o[:, TILE : 2 * TILE] = left[BLOCK : 2 * BLOCK]
    coef_o[3] = (p02 + r2)[:, :BLOCK]
    coef_o[4] = transposed(upper3)[:, :BLOCK]
    for n, part in pending:
        pltpu.make_async_copy(part, part, send_sem.at[n]).wait()


def hand_over(left_i, right_i, coef_i, left_o, right_o, coef_o):
    left_o[...] = left_i[...]
    right_o[...] = right_i[...]
    coef_o[...] = coef_i[...]


def on_device(tiles, tile_rows, tile_cols, counts, start_block):
    anywhere = pl.BlockSpec(memory_space=pl.ANY)
    vmem = pl.BlockSpec(memory_space=pltpu.VMEM)
    shapes = (
        jax.ShapeDtypeStruct((BLOCK, DOC_TILES * TILE // NT), F32),
        jax.ShapeDtypeStruct((BLOCK, TERM_TILES * TILE // ND), F32),
        jax.ShapeDtypeStruct((5, BLOCK, BLOCK), F32),
    )
    results = pl.pallas_call(
        kernel,
        out_shape=shapes,
        in_specs=[anywhere] * 5,
        out_specs=(vmem, vmem, vmem),
        scratch_shapes=[
            pltpu.SMEM((1, 1), jnp.int32),
            pltpu.SMEM((1, SLOTS), jnp.int32),
            pltpu.SMEM((1, SLOTS), jnp.int32),
            pltpu.VMEM((SLOTS, TILE, TILE), BF16),
            pltpu.VMEM((TERM_TILES, BLOCK, TILE), F32),
            pltpu.VMEM((DOC_TILES * BLOCK, NT * LANES), BF16),
            pltpu.VMEM((TERM_TILES * BLOCK, ND * LANES), BF16),
            pltpu.VMEM((NT, 24, LANES), F32),
            pltpu.VMEM((ND, 16, LANES), F32),
            pltpu.VMEM((ND, SLOTS, TILE), F32),
            pltpu.VMEM((4, NT, TX, LANES), F32),
            pltpu.VMEM((4, NT, TX, LANES), F32),
            pltpu.VMEM((2, ND, DX, LANES), F32),
            pltpu.VMEM((3, ND, DX, LANES), F32),
            pltpu.VMEM((3, ND, 8, LANES), F32),
            pltpu.VMEM((3, NT, 8, LANES), F32),
            pltpu.VMEM((TILE, LANES), F32),
            pltpu.VMEM((TGROUPS, LANES, LANES), F32),
            pltpu.VMEM((TILE, ND * SLOTS), F32),
            pltpu.VMEM((DGROUPS, SLOTS, LANES), F32),
            pltpu.VMEM((NT, SLOTS, LANES), F32),
            pltpu.VMEM((LANES, LANES), F32),
            pltpu.VMEM((2, NT, 8, LANES), F32),
            pltpu.VMEM((2, NT, 8, LANES), F32),
            pltpu.SemaphoreType.DMA((SLOTS + 4,)),
            pltpu.SemaphoreType.DMA((18,)),
            pltpu.SemaphoreType.DMA((18, 2)),
        ],
        compiler_params=pltpu.CompilerParams(
            collective_id=0, has_side_effects=True, vmem_limit_bytes=56000000
        ),
    )(
        counts,
        tile_rows.reshape(1, SLOTS),
        tile_cols.reshape(1, SLOTS),
        tiles.reshape(SLOTS, TILE, TILE),
        start_block,
    )
    return pl.pallas_call(
        hand_over,
        out_shape=shapes,
        in_specs=[vmem, vmem, vmem],
        out_specs=(vmem, vmem, vmem),
        compiler_params=pltpu.CompilerParams(vmem_limit_bytes=8 * 1024 * 1024),
    )(*results)


def solution(mesh):
    return jax.shard_map(
        on_device,
        mesh=mesh,
        in_specs=(
            P("doc", "term", None, None, None),
            P("doc", "term", None),
            P("doc", "term", None),
            P("doc", "term"),
            P(None, "term"),
        ),
        out_specs=(P(None, ("doc", "term")), P(None, ("term", "doc")), P()),
        check_vma=False,
    )
```

```python
import functools

import jax
import jax.numpy as jnp
from jax import lax
from jax.experimental import pallas as pl
from jax.experimental.pallas import tpu as pltpu
from jax.sharding import PartitionSpec as P

MESH = pl.DeviceIdType.MESH
F32 = jnp.float32
BF16 = jnp.bfloat16
TILE = 512
BLOCK = 16
SLOTS = 8
LANES = SLOTS * BLOCK
TERM_TILES = 64
DOC_TILES = 32
ND = 8
NT = 16
DX = TILE // ND
TX = TILE // NT
DGROUPS = DOC_TILES * BLOCK // LANES
TGROUPS = TERM_TILES * BLOCK // LANES
N_DOCS = ND * DOC_TILES * TILE
N_TERMS = NT * TERM_TILES * TILE
HIGHEST = lax.Precision.HIGHEST


def dot(a, b, contract, precision=HIGHEST):
    return lax.dot_general(
        a, b, (contract, ((), ())), precision=precision, preferred_element_type=F32
    )


NN = ((1,), (0,))
NTR = ((1,), (1,))
TN = ((0,), (0,))


def halves(x):
    hi = x.astype(BF16)
    lo = (x - hi.astype(F32)).astype(BF16)
    return jnp.concatenate([hi, lo], axis=0)


def iota(shape, dim):
    return lax.broadcasted_iota(jnp.int32, shape, dim)


def roll(x, shift):
    return pltpu.roll(x, shift, 1)


def fold(t):
    same = iota((LANES, LANES), 0) // BLOCK == iota((LANES, LANES), 1) // BLOCK
    t = jnp.where(same, t, 0.0)
    w = t[0:BLOCK]
    for g in range(1, SLOTS):
        w = w + t[g * BLOCK : (g + 1) * BLOCK]
    w = w + roll(w, 64)
    w = w + roll(w, 32)
    return w + roll(w, 16)


def packed(s, r):
    group = iota((8, LANES), 1) // BLOCK
    z = jnp.where(group == 0, s[0:8], s[8:16])
    if r is None:
        return z
    return jnp.where(group < 2, z, jnp.where(group == 2, r[0:8], r[8:16]))


def unpacked(z, first):
    lane = iota((BLOCK, LANES), 1)
    top = z if first == 0 else roll(z, LANES - BLOCK * first)
    low = roll(z, LANES - BLOCK * (first + 1))
    return jnp.where(lane < BLOCK, jnp.concatenate([top, low], axis=0), 0.0)


def spread(m):
    same = iota((LANES, LANES), 0) // BLOCK == iota((LANES, LANES), 1) // BLOCK
    r = m + roll(m, 16)
    r = r + roll(r, 32)
    r = r + roll(r, 64)
    return jnp.where(same, jnp.concatenate([r] * SLOTS, axis=0), 0.0)


def factor(s):
    lane = iota((BLOCK, LANES), 1)
    sub = iota((BLOCK, LANES), 0)
    m = jnp.where(lane < BLOCK, s, jnp.where(lane == sub + BLOCK, 1.0, 0.0))
    for c in range(BLOCK - 1):
        ratio = m[c : c + 1, :] / m[c : c + 1, c : c + 1]
        m = m - jnp.where(sub > c, m[:, c : c + 1], 0.0) * ratio
    diag = jnp.sum(jnp.where(lane == sub, m, 0.0), axis=1, keepdims=True)
    m = m * lax.rsqrt(diag)
    upper = jnp.where((lane < BLOCK) & (lane >= sub), m, 0.0)
    inverse = jnp.where(lane < BLOCK, roll(m, LANES - BLOCK), 0.0)
    return upper, inverse


def transposed(m):
    full = jnp.concatenate([m, jnp.zeros((LANES - BLOCK, LANES), F32)], axis=0)
    return full.T[:BLOCK, :]


def kernel(
    cnt_h, rows_h, cols_h, tiles_h, start_h,
    left_o, right_o, coef_o,
    cnt_s, rows_s, cols_s, tiles_v, start_v, st_v, sd_v,
    m1_v, d1_v, cs_v,
    tsend, trecv, dsend, drecv, za, zb,
    slots_v, share_v, cst_v, rs_v, rsr_v, rst_v, pk_v, pkr_v,
    load_sem, send_sem, recv_sem,
):
    i = lax.axis_index("doc")
    j = lax.axis_index("term")
    bar = pltpu.get_barrier_semaphore()
    for d in range(1, NT):
        pl.semaphore_signal(bar, 1, device_id=(i, lax.rem(j + d, NT)), device_id_type=MESH)
    for d in range(1, ND):
        pl.semaphore_signal(bar, 1, device_id=(lax.rem(i + d, ND), j), device_id_type=MESH)

    def load_start(t, carry):
        columns = pl.ds(pl.multiple_of(t * TILE, TILE), TILE)
        pltpu.make_async_copy(start_h.at[:, columns], start_v.at[t], load_sem.at[SLOTS]).start()
        return carry

    lax.fori_loop(0, TERM_TILES, load_start, 0)
    rows_load = pltpu.make_async_copy(rows_h, rows_s, load_sem.at[SLOTS + 1])
    cols_load = pltpu.make_async_copy(cols_h, cols_s, load_sem.at[SLOTS + 2])
    cnt_load = pltpu.make_async_copy(cnt_h, cnt_s, load_sem.at[SLOTS + 3])
    cnt_load.start()
    rows_load.start()
    cols_load.start()
    loads = []
    for k in range(SLOTS):
        load = pltpu.make_async_copy(tiles_h.at[k], tiles_v.at[k], load_sem.at[k])
        load.start()
        loads.append(load)

    pending = []

    def to_terms(n, src_of, dst):
        def send(d, carry):
            q = lax.rem(j + d, NT)
            pltpu.make_async_remote_copy(
                src_ref=src_of(q), dst_ref=dst.at[j],
                send_sem=send_sem.at[n], recv_sem=recv_sem.at[n, 0],
                device_id=(i, q), device_id_type=MESH,
            ).start()
            return carry
        lax.fori_loop(1, NT, send, 0)
        pending.append((n, dst.at[pl.ds(0, NT - 1)]))

    def to_docs(n, src_of, dst):
        def send(d, carry):
            q = lax.rem(i + d, ND)
            pltpu.make_async_remote_copy(
                src_ref=src_of(q), dst_ref=dst.at[i],
                send_sem=send_sem.at[n], recv_sem=recv_sem.at[n, 0],
                device_id=(q, j), device_id_type=MESH,
            ).start()
            return carry
        lax.fori_loop(1, ND, send, 0)
        pending.append((n, dst.at[pl.ds(0, ND - 1)]))

    def arrived(n, dst, peers, group=0):
        part = dst.at[pl.ds(0, peers - 1)]
        pltpu.make_async_copy(part, part, recv_sem.at[n, group]).wait()

    y = j // 4
    t0 = lax.rem(j, 4)
    xl = i // 4
    z0 = lax.rem(i, 4)

    def term_block_send(n, slot, block, dy, looped=False):
        yb = lax.rem(y + dy, 4)
        tsend[slot, pl.ds(4 * yb, 4)] = block.reshape(4, TX, LANES)
        if dy == 0:
            trecv[slot, j] = tsend[slot, j]
            pending.append((n, trecv.at[slot, pl.ds(0, NT - 1)]))

        def send(t, carry=0):
            q = 4 * yb + lax.rem(t0 + t, 4)
            pltpu.make_async_remote_copy(
                src_ref=tsend.at[slot, q], dst_ref=trecv.at[slot, j],
                send_sem=send_sem.at[n], recv_sem=recv_sem.at[n, 1 if dy == 2 else 0],
                device_id=(i, q), device_id_type=MESH,
            ).start()
            return carry

        if looped:
            lax.fori_loop(1, 4 if dy == 0 else 5, send, 0)
        else:
            for t in (2, 3, 1) if dy == 0 else (2, 3, 1, 0):
                send(t)

    def doc_block_send(n, slot, block, dx, looped=False):
        xb = lax.rem(xl + dx, 2)
        dsend[slot, pl.ds(4 * xb, 4)] = block.reshape(4, DX, LANES)
        if dx == 0:
            drecv[slot, i] = dsend[slot, i]
            pending.append((n, drecv.at[slot, pl.ds(0, ND - 1)]))

        def send(t, carry=0):
            q = 4 * xb + lax.rem(z0 + t, 4)
            pltpu.make_async_remote_copy(
                src_ref=dsend.at[slot, q], dst_ref=drecv.at[slot, i],
                send_sem=send_sem.at[n], recv_sem=recv_sem.at[n, dx],
                device_id=(q, j), device_id_type=MESH,
            ).start()
            return carry

        if looped:
            lax.fori_loop(1, 4 if dx == 0 else 5, send, 0)
        else:
            for t in (2, 1, 3) if dx == 0 else (2, 1, 3, 0):
                send(t)

    def forward_exchange(n, slot, x):
        lane_slot = iota((TILE, LANES), 1) // BLOCK
        weights = []
        for k in range(SLOTS):
            masked = [jnp.where(lane_slot == k, part, 0.0).astype(BF16) for part in x]
            weights.append(masked[0] if len(masked) == 1 else jnp.concatenate(masked, axis=1))
        for pair in ((2, 1), (3, 0)):
            rows = [pl.ds(pl.multiple_of(128 * lax.rem(y + dy, 4), 128), 128) for dy in pair]
            total = None
            for k in range(SLOTS):
                lhs = jnp.concatenate([tiles_v[k, r, :] for r in rows], axis=0)
                part = dot(lhs, weights[k], NN, None)
                total = part if total is None else total + part
            if len(x) == 2:
                total = total[:, :LANES] + total[:, LANES:]
            term_block_send(n, slot, total[:128], pair[0])
            term_block_send(n, slot, total[128:], pair[1])

    def term_sum(n, slot):
        acc = None
        for rel in (0, 1, 3, 2):
            if rel == 0:
                arrived(n, trecv.at[slot], 12)
            if rel == 2:
                arrived(n, trecv.at[slot], 5, 1)
            yb = lax.rem(y + rel, 4)
            block = trecv[slot, pl.ds(4 * yb, 4)]
            flat = jnp.concatenate([block[t] for t in range(4)], axis=1)
            onehot = st_v[:, pl.ds(pl.multiple_of(512 * yb, 512), 512)]
            part = dot(halves(flat), onehot, NTR, None)
            acc = part if acc is None else acc + part
        return acc[:TX] + acc[TX:]

    def term_gather(n, slot, x):
        both = halves(x)
        for dy in (2, 1, 3, 0):
            yb = lax.rem(y + dy, 4)
            part = dot(both, st_v[:, pl.ds(pl.multiple_of(512 * yb, 512), 512)], NN, None)
            term_block_send(n, slot, stacked(part[:TX] + part[TX:], 4), dy, dy in (0, 2))

    def doc_sum(n, slot):
        acc = None
        for dx in (0, 1):
            arrived(n, drecv.at[slot], 4 + dx, dx)
            xb = lax.rem(xl + dx, 2)
            block = drecv[slot, pl.ds(4 * xb, 4)]
            flat = jnp.concatenate([block[t] for t in range(4)], axis=1)
            onehot = sd_v[:, pl.ds(pl.multiple_of(512 * xb, 512), 512)]
            part = dot(halves(flat), onehot, NTR, None)
            acc = part if acc is None else acc + part
        return acc[:DX] + acc[DX:]

    def doc_gather(n, slot, x):
        both = halves(x)
        for dx in (1, 0):
            xb = lax.rem(xl + dx, 2)
            part = dot(both, sd_v[:, pl.ds(pl.multiple_of(512 * xb, 512), 512)], NN, None)
            doc_block_send(n, slot, stacked(part[:DX] + part[DX:], 4), dx, True)

    def split(x):
        hi = x.astype(BF16).astype(F32)
        return [hi, x - hi]

    def stacked(x, groups):
        return jnp.concatenate([x[:, g * LANES : (g + 1) * LANES] for g in range(groups)], axis=0)

    def flat_of(x, groups):
        n = x.shape[0] // groups
        return jnp.concatenate([x[g * n : (g + 1) * n] for g in range(groups)], axis=1)

    def pack(x, out):
        group = iota((8, LANES), 1) // (2 * BLOCK)
        for g in range(DGROUPS):
            rows = [x[g * TX + 8 * h : g * TX + 8 * (h + 1)] for h in range(4)]
            for m in range(4):
                total = None
                for h in range(4):
                    shift = (32 * (h - m)) % LANES
                    turned = rows[h] if shift == 0 else roll(rows[h], shift)
                    total = turned if total is None else jnp.where(group == h, turned, total)
                out[4 * g + m] = total

    def unpack(ref):
        rows = []
        for q in range(NT):
            for h in range(4):
                rows.append(ref[q] if h == 0 else roll(ref[q], LANES - 32 * h))
        return jnp.concatenate(rows, axis=0)

    def all_sum(n, base, z):
        za[n, i] = z
        to_docs(base, lambda q: za.at[n, i], za.at[n])

        def rest():
            arrived(base, za.at[n], ND)
            s = za[n, 0]
            for q in range(1, ND):
                s = s + za[n, q]
            zb[n, j] = s
            to_terms(base + 1, lambda q: zb.at[n, j], zb.at[n])

        def last():
            arrived(base + 1, zb.at[n], NT)
            s = zb[n, 0]
            for q in range(1, NT):
                s = s + zb[n, q]
            return s

        return rest, last

    pltpu.make_async_copy(start_v, start_v, load_sem.at[SLOTS]).wait()
    acc = jnp.zeros((2 * LANES, 2 * LANES), F32)
    for ch in range(8):
        both = halves(start_v[ch * 8 : (ch + 1) * 8].reshape(LANES, TILE))
        acc = acc + dot(both, both, NTR, None)
    t = acc[:LANES, :LANES] + acc[:LANES, LANES:] + acc[LANES:, :LANES] + acc[LANES:, LANES:]
    start_gram = packed(fold(t) * (1.0 / N_TERMS), None)

    cnt_load.wait()
    rows_load.wait()
    cols_load.wait()
    lane8 = iota((8, LANES), 1)
    sub8 = iota((8, LANES), 0)
    cnt = cnt_s[0, 0]
    row_at = jnp.zeros((8, LANES), jnp.int32)
    my_col = jnp.zeros((8, LANES), jnp.int32)
    col_of = jnp.zeros((8, LANES), jnp.int32)
    row_of = jnp.zeros((8, LANES), jnp.int32)
    for k in range(SLOTS):
        here = lane8 // BLOCK == k
        row_at = jnp.where(here, rows_s[0, k] * BLOCK, row_at)
        my_col = jnp.where(here, cols_s[0, k], my_col)
        col_of = jnp.where(sub8 == k, cols_s[0, k], col_of)
        row_of = jnp.where(sub8 == k, rows_s[0, k], row_of)
    row_at = jnp.where(lane8 // BLOCK < cnt, row_at, -100000)
    my_col = jnp.where(lane8 // BLOCK < cnt, my_col, -10000)
    col_of = jnp.where(sub8 < cnt, col_of, -10000)
    row_of = jnp.where(sub8 < cnt, row_of, -10000)
    col_at = my_col * BLOCK
    row_at = (row_at + lane8 % BLOCK).astype(F32)
    col_at = (col_at + lane8 % BLOCK).astype(F32)
    my_col = my_col.astype(F32)
    d1_v[i] = jnp.concatenate([col_of.astype(F32), col_at], axis=0)
    m1_v[j] = jnp.concatenate([start_gram, row_at, row_of.astype(F32)], axis=0)

    col_sums = jnp.zeros((16, TILE), F32)
    for k in range(SLOTS):
        loads[k].wait()
        ones = jnp.where(iota((16, TILE), 0) == k, 1.0, 0.0).astype(BF16)
        col_sums = col_sums + dot(ones, tiles_v[k], NN, None)
    cs_v[i] = col_sums[:SLOTS]

    pl.semaphore_wait(bar, ND - 1 + NT - 1)
    to_terms(2, lambda q: m1_v.at[j], m1_v)
    to_docs(0, lambda q: d1_v.at[i], d1_v)
    to_docs(1, lambda q: cs_v.at[i], cs_v)

    row_sums = jnp.zeros((16, TILE), F32)
    for k in range(SLOTS):
        ones = jnp.where(iota((16, TILE), 0) == k, 1.0, 0.0).astype(BF16)
        row_sums = row_sums + dot(ones, tiles_v[k], NTR, None)
    for g in range(DGROUPS):
        rs_v[g] = row_sums[:SLOTS, g * LANES : (g + 1) * LANES]
    rsr_v[j] = rs_v[j // 4]
    to_terms(3, lambda q: rs_v.at[q // 4], rsr_v)
    slots_t = jnp.concatenate([start_v[cols_s[0, k]] for k in range(SLOTS)], axis=0).T
    slots_v[...] = slots_t

    arrived(0, d1_v, ND)
    arrived(1, cs_v, ND)
    arrived(2, m1_v, NT)
    cols_in = jnp.concatenate([d1_v[q, 0:8, :] for q in range(ND)], axis=0)
    sums_t = jnp.concatenate([cs_v[q] for q in range(ND)], axis=0).T
    cst_v[...] = sums_t
    same_col = jnp.where(cols_in == my_col[0:1, :], 1.0, 0.0)
    col_scale = lax.rsqrt(dot(sums_t, same_col, NN) + 1.0)
    scaled_slots = slots_v[...] * col_scale
    gram = m1_v[0, 0:8, :]
    for q in range(1, NT):
        gram = gram + m1_v[q, 0:8, :]
    _, inverse0 = factor(unpacked(gram, 0))
    k0 = spread(inverse0)
    forward_exchange(4, 1, [dot(scaled_slots, k0, NTR)])

    for q in range(NT):
        hit = iota((DOC_TILES * BLOCK, LANES), 0).astype(F32) == m1_v[q, 8:9, :]
        st_v[:, q * LANES : (q + 1) * LANES] = jnp.where(hit, 1.0, 0.0).astype(BF16)
    rows_in = jnp.concatenate([m1_v[q, 16:24, :] for q in range(NT)], axis=0)
    rows_wide = jnp.concatenate([rows_in] * DGROUPS, axis=1)
    row_tile = (iota((LANES, DOC_TILES * BLOCK), 1) // BLOCK).astype(F32)
    same_row = jnp.where(rows_wide == row_tile, 1.0, 0.0)
    arrived(3, rsr_v, NT)
    rst_v[...] = jnp.concatenate([rsr_v[q] for q in range(NT)], axis=0).T
    my_rows = rst_v[pl.ds(pl.multiple_of(TX * lax.rem(j, 4), TX), TX), :]
    row_scale = lax.rsqrt(dot(my_rows, same_row, NN) + 1.0)
    row_square = row_scale * row_scale

    image = term_sum(4, 1)
    term_gather(5, 2, image * row_square)
    f0 = stacked(image * row_scale, DGROUPS)
    rest, last = all_sum(0, 6, packed(fold(dot(f0, f0, TN)) * (1.0 / N_DOCS), None))
    pack(f0, pk_v.at[0])
    pkr_v[0, j] = pk_v[0, j]
    to_terms(8, lambda q: pk_v.at[0, q], pkr_v.at[0])

    for q in range(ND):
        hit = iota((TERM_TILES * BLOCK, LANES), 0).astype(F32) == d1_v[q, 8:9, :]
        sd_v[:, q * LANES : (q + 1) * LANES] = jnp.where(hit, 1.0, 0.0).astype(BF16)
    rest()
    arrived(5, trecv.at[2], 12)
    arrived(5, trecv.at[2], 5, 1)
    pieces = jnp.concatenate([trecv[2, q] for q in range(NT)], axis=0).T
    hi = pieces.astype(BF16)
    lo = (pieces - hi.astype(F32)).astype(BF16)
    pairs = []
    for k in range(SLOTS):
        part = slice(k * BLOCK, (k + 1) * BLOCK)
        pairs.append(jnp.concatenate([hi[part], lo[part]], axis=0))
    for dx in (1, 0):
        columns = pl.ds(pl.multiple_of(256 * lax.rem(xl + dx, 2), 256), 256)
        back = []
        for k in range(SLOTS):
            both = dot(pairs[k], tiles_v[k, :, columns], NN, None)
            back.append(both[:BLOCK] + both[BLOCK:])
        doc_block_send(9, 0, jnp.concatenate(back, axis=0).T, dx)

    cols_wide = jnp.concatenate([cols_in] * TGROUPS, axis=1)
    tile_at = (iota((ND * SLOTS, TERM_TILES * BLOCK), 1) // BLOCK).astype(F32)
    my_sums = cst_v[pl.ds(pl.multiple_of(i * DX, DX), DX), :]
    col_share = lax.rsqrt(dot(my_sums, jnp.where(cols_wide == tile_at, 1.0, 0.0), NN) + 1.0)
    col_square = col_share * col_share
    window = pl.ds(pl.multiple_of(128 * (i // 2), 128), 128)
    for g in range(TGROUPS):
        share_v[g] = start_v[g * 8 : (g + 1) * 8, :, window].reshape(LANES, 128).T
    half = pl.multiple_of(DX * lax.rem(i, 2), DX)
    start_share = jnp.concatenate([share_v[g, pl.ds(half, DX), :] for g in range(TGROUPS)], axis=0)
    e_share = dot(start_share, k0, NTR)
    upper1, inverse1 = factor(unpacked(last(), 0))
    k1 = spread(inverse1)
    p0 = upper1 * (N_DOCS / N_TERMS)
    expected = dot(e_share, spread(p0), NTR)
    u1 = dot(f0, k1, NTR)

    image = doc_sum(9, 0)
    doc_gather(10, 1, image * col_square)
    b1 = dot(stacked(image * col_share, TGROUPS), k1, NTR) - expected
    t2 = dot(b1, jnp.concatenate([b1, e_share], axis=1), TN) * (1.0 / N_TERMS)
    rest, last = all_sum(1, 11, packed(fold(t2[:, :LANES]), fold(t2[:, LANES:])))
    for g in range(TGROUPS):
        share_v[g, 0:DX, :] = b1[g * DX : (g + 1) * DX]
    drecv[2, i] = share_v[i, 0:DX, :]

    rest()
    arrived(10, drecv.at[1], 4)
    arrived(10, drecv.at[1], 5, 1)
    pieces = jnp.concatenate([drecv[1, q] for q in range(ND)], axis=0)
    forward_exchange(14, 3, split(pieces))
    to_docs(13, lambda q: share_v.at[q, pl.ds(0, DX), :], drecv.at[2])
    z = last()
    r1 = unpacked(z, 2)
    pad = jnp.zeros((LANES - BLOCK, LANES), F32)
    g2 = unpacked(z, 0) - dot(r1, jnp.concatenate([r1, pad], axis=0), NTR)
    upper2, inverse2 = factor(g2)
    k2 = spread(inverse2)
    kr1 = spread(r1)
    p02 = upper2 * (N_TERMS / N_DOCS)
    k21 = dot(k2, k1, NN)
    known = dot(k2, spread(p0 + r1), NN) + dot(spread(p02), k1, NN)
    expected = dot(f0, known, NTR)

    image = term_sum(14, 3) * row_scale
    x2 = dot(stacked(image, DGROUPS), k21, NTR) - expected
    t3 = dot(x2, jnp.concatenate([x2, u1], axis=1), TN) * (1.0 / N_DOCS)
    rest, last = all_sum(2, 15, packed(fold(t3[:, :LANES]), fold(t3[:, LANES:])))
    pack(x2, pk_v.at[1])
    pkr_v[1, j] = pk_v[1, j]
    to_terms(17, lambda q: pk_v.at[1, q], pkr_v.at[1])
    rest()
    arrived(13, drecv.at[2], ND)
    right_x = jnp.concatenate([drecv[2, q] for q in range(ND)], axis=0)

    start_st = start_v[pl.ds(i * 8, 8)].reshape(LANES, TILE)
    k20 = dot(k2, dot(kr1, k0, NN), NN)
    right = dot(k2, right_x, NTR) - dot(k20, start_st, NN)
    for g in range(8):
        right_o[:, g * TILE : (g + 1) * TILE] = right[g * BLOCK : (g + 1) * BLOCK]
    coef_o[0] = transposed(upper1)[:, :BLOCK]
    coef_o[1] = (p0 + r1)[:, :BLOCK]
    coef_o[2] = transposed(upper2)[:, :BLOCK]
    arrived(8, pkr_v.at[0], NT)
    left_u = dot(unpack(pkr_v.at[0]), k1, NTR)
    arrived(17, pkr_v.at[1], NT)
    left_x = unpack(pkr_v.at[1])

    z = last()
    r2 = unpacked(z, 2)
    g3 = unpacked(z, 0) - dot(r2, jnp.concatenate([r2, pad], axis=0), NTR)
    upper3, inverse3 = factor(g3)
    left_x = left_x - dot(left_u, spread(r2), NTR)
    rep = inverse3 + roll(inverse3, 16)
    rep = rep + roll(rep, 32)
    rep = rep + roll(rep, 64)
    mine = iota((2 * BLOCK, LANES), 1) // BLOCK == iota((2 * BLOCK, LANES), 0) // BLOCK
    left = dot(jnp.where(mine, jnp.concatenate([rep, rep], axis=0), 0.0), left_x, NTR)
    left_o[:, 0:TILE] = left[0:BLOCK]
    left_o[:, TILE : 2 * TILE] = left[BLOCK : 2 * BLOCK]
    coef_o[3] = (p02 + r2)[:, :BLOCK]
    coef_o[4] = transposed(upper3)[:, :BLOCK]
    for n, part in pending:
        pltpu.make_async_copy(part, part, send_sem.at[n]).wait()


def hand_over(left_i, right_i, coef_i, left_o, right_o, coef_o):
    left_o[...] = left_i[...]
    right_o[...] = right_i[...]
    coef_o[...] = coef_i[...]


def on_device(tiles, tile_rows, tile_cols, counts, start_block):
    anywhere = pl.BlockSpec(memory_space=pl.ANY)
    vmem = pl.BlockSpec(memory_space=pltpu.VMEM)
    shapes = (
        jax.ShapeDtypeStruct((BLOCK, DOC_TILES * TILE // NT), F32),
        jax.ShapeDtypeStruct((BLOCK, TERM_TILES * TILE // ND), F32),
        jax.ShapeDtypeStruct((5, BLOCK, BLOCK), F32),
    )
    results = pl.pallas_call(
        kernel,
        out_shape=shapes,
        in_specs=[anywhere] * 5,
        out_specs=(vmem, vmem, vmem),
        scratch_shapes=[
            pltpu.SMEM((1, 1), jnp.int32),
            pltpu.SMEM((1, SLOTS), jnp.int32),
            pltpu.SMEM((1, SLOTS), jnp.int32),
            pltpu.VMEM((SLOTS, TILE, TILE), BF16),
            pltpu.VMEM((TERM_TILES, BLOCK, TILE), F32),
            pltpu.VMEM((DOC_TILES * BLOCK, NT * LANES), BF16),
            pltpu.VMEM((TERM_TILES * BLOCK, ND * LANES), BF16),
            pltpu.VMEM((NT, 24, LANES), F32),
            pltpu.VMEM((ND, 16, LANES), F32),
            pltpu.VMEM((ND, SLOTS, TILE), F32),
            pltpu.VMEM((4, NT, TX, LANES), F32),
            pltpu.VMEM((4, NT, TX, LANES), F32),
            pltpu.VMEM((2, ND, DX, LANES), F32),
            pltpu.VMEM((3, ND, DX, LANES), F32),
            pltpu.VMEM((3, ND, 8, LANES), F32),
            pltpu.VMEM((3, NT, 8, LANES), F32),
            pltpu.VMEM((TILE, LANES), F32),
            pltpu.VMEM((TGROUPS, LANES, LANES), F32),
            pltpu.VMEM((TILE, ND * SLOTS), F32),
            pltpu.VMEM((DGROUPS, SLOTS, LANES), F32),
            pltpu.VMEM((NT, SLOTS, LANES), F32),
            pltpu.VMEM((LANES, LANES), F32),
            pltpu.VMEM((2, NT, 8, LANES), F32),
            pltpu.VMEM((2, NT, 8, LANES), F32),
            pltpu.SemaphoreType.DMA((SLOTS + 4,)),
            pltpu.SemaphoreType.DMA((18,)),
            pltpu.SemaphoreType.DMA((18, 2)),
        ],
        compiler_params=pltpu.CompilerParams(
            collective_id=0, has_side_effects=True, vmem_limit_bytes=56000000
        ),
    )(
        counts,
        tile_rows.reshape(1, SLOTS),
        tile_cols.reshape(1, SLOTS),
        tiles.reshape(SLOTS, TILE, TILE),
        start_block,
    )
    return pl.pallas_call(
        hand_over,
        out_shape=shapes,
        in_specs=[vmem, vmem, vmem],
        out_specs=(vmem, vmem, vmem),
        compiler_params=pltpu.CompilerParams(vmem_limit_bytes=8 * 1024 * 1024),
    )(*results)


def solution(mesh):
    return jax.shard_map(
        on_device,
        mesh=mesh,
        in_specs=(
            P("doc", "term", None, None, None),
            P("doc", "term", None),
            P("doc", "term", None),
            P("doc", "term"),
            P(None, "term"),
        ),
        out_specs=(P(None, ("doc", "term")), P(None, ("term", "doc")), P()),
        check_vma=False,
    )
```

```python
import functools

import jax
import jax.numpy as jnp
from jax import lax
from jax.experimental import pallas as pl
from jax.experimental.pallas import tpu as pltpu
from jax.sharding import PartitionSpec as P

MESH = pl.DeviceIdType.MESH
F32 = jnp.float32
BF16 = jnp.bfloat16
TILE = 512
BLOCK = 16
SLOTS = 8
LANES = SLOTS * BLOCK
TERM_TILES = 64
DOC_TILES = 32
ND = 8
NT = 16
DX = TILE // ND
TX = TILE // NT
DGROUPS = DOC_TILES * BLOCK // LANES
TGROUPS = TERM_TILES * BLOCK // LANES
N_DOCS = ND * DOC_TILES * TILE
N_TERMS = NT * TERM_TILES * TILE
HIGHEST = lax.Precision.HIGHEST


def dot(a, b, contract, precision=HIGHEST):
    return lax.dot_general(
        a, b, (contract, ((), ())), precision=precision, preferred_element_type=F32
    )


NN = ((1,), (0,))
NTR = ((1,), (1,))
TN = ((0,), (0,))


def halves(x):
    hi = x.astype(BF16)
    lo = (x - hi.astype(F32)).astype(BF16)
    return jnp.concatenate([hi, lo], axis=0)


def iota(shape, dim):
    return lax.broadcasted_iota(jnp.int32, shape, dim)


def roll(x, shift):
    return pltpu.roll(x, shift, 1)


def fold(t):
    same = iota((LANES, LANES), 0) // BLOCK == iota((LANES, LANES), 1) // BLOCK
    t = jnp.where(same, t, 0.0)
    w = t[0:BLOCK]
    for g in range(1, SLOTS):
        w = w + t[g * BLOCK : (g + 1) * BLOCK]
    w = w + roll(w, 64)
    w = w + roll(w, 32)
    return w + roll(w, 16)


def packed(s, r):
    group = iota((8, LANES), 1) // BLOCK
    z = jnp.where(group == 0, s[0:8], s[8:16])
    if r is None:
        return z
    return jnp.where(group < 2, z, jnp.where(group == 2, r[0:8], r[8:16]))


def unpacked(z, first):
    lane = iota((BLOCK, LANES), 1)
    top = z if first == 0 else roll(z, LANES - BLOCK * first)
    low = roll(z, LANES - BLOCK * (first + 1))
    return jnp.where(lane < BLOCK, jnp.concatenate([top, low], axis=0), 0.0)


def spread(m):
    same = iota((LANES, LANES), 0) // BLOCK == iota((LANES, LANES), 1) // BLOCK
    r = m + roll(m, 16)
    r = r + roll(r, 32)
    r = r + roll(r, 64)
    return jnp.where(same, jnp.concatenate([r] * SLOTS, axis=0), 0.0)


def factor(s):
    lane = iota((BLOCK, LANES), 1)
    sub = iota((BLOCK, LANES), 0)
    m = jnp.where(lane < BLOCK, s, jnp.where(lane == sub + BLOCK, 1.0, 0.0))
    for c in range(BLOCK - 1):
        ratio = m[c : c + 1, :] / m[c : c + 1, c : c + 1]
        m = m - jnp.where(sub > c, m[:, c : c + 1], 0.0) * ratio
    diag = jnp.sum(jnp.where(lane == sub, m, 0.0), axis=1, keepdims=True)
    m = m * lax.rsqrt(diag)
    upper = jnp.where((lane < BLOCK) & (lane >= sub), m, 0.0)
    inverse = jnp.where(lane < BLOCK, roll(m, LANES - BLOCK), 0.0)
    return upper, inverse


def transposed(m):
    full = jnp.concatenate([m, jnp.zeros((LANES - BLOCK, LANES), F32)], axis=0)
    return full.T[:BLOCK, :]


def kernel(
    cnt_h, rows_h, cols_h, tiles_h, start_h,
    left_o, right_o, coef_o,
    cnt_s, rows_s, cols_s, tiles_v, start_v, st_v, sd_v,
    m1_v, d1_v, cs_v,
    tsend, trecv, dsend, drecv, za, zb,
    slots_v, share_v, cst_v, rs_v, rsr_v, rst_v, pk_v, pkr_v,
    load_sem, send_sem, recv_sem,
):
    i = lax.axis_index("doc")
    j = lax.axis_index("term")
    bar = pltpu.get_barrier_semaphore()
    for d in range(1, NT):
        pl.semaphore_signal(bar, 1, device_id=(i, lax.rem(j + d, NT)), device_id_type=MESH)
    for d in range(1, ND):
        pl.semaphore_signal(bar, 1, device_id=(lax.rem(i + d, ND), j), device_id_type=MESH)

    def load_start(t, carry):
        columns = pl.ds(pl.multiple_of(t * TILE, TILE), TILE)
        pltpu.make_async_copy(start_h.at[:, columns], start_v.at[t], load_sem.at[SLOTS]).start()
        return carry

    lax.fori_loop(0, TERM_TILES, load_start, 0)
    rows_load = pltpu.make_async_copy(rows_h, rows_s, load_sem.at[SLOTS + 1])
    cols_load = pltpu.make_async_copy(cols_h, cols_s, load_sem.at[SLOTS + 2])
    cnt_load = pltpu.make_async_copy(cnt_h, cnt_s, load_sem.at[SLOTS + 3])
    cnt_load.start()
    rows_load.start()
    cols_load.start()
    loads = []
    for k in range(SLOTS):
        load = pltpu.make_async_copy(tiles_h.at[k], tiles_v.at[k], load_sem.at[k])
        load.start()
        loads.append(load)

    pending = []

    def to_terms(n, src_of, dst):
        def send(d, carry):
            q = lax.rem(j + lax.rem(d + 6, NT - 1) + 1, NT)
            pltpu.make_async_remote_copy(
                src_ref=src_of(q), dst_ref=dst.at[j],
                send_sem=send_sem.at[n], recv_sem=recv_sem.at[n, 0],
                device_id=(i, q), device_id_type=MESH,
            ).start()
            return carry
        lax.fori_loop(1, NT, send, 0)
        pending.append((n, dst.at[pl.ds(0, NT - 1)]))

    def to_docs(n, src_of, dst):
        def send(d, carry):
            q = lax.rem(i + lax.rem(d + 2, ND - 1) + 1, ND)
            pltpu.make_async_remote_copy(
                src_ref=src_of(q), dst_ref=dst.at[i],
                send_sem=send_sem.at[n], recv_sem=recv_sem.at[n, 0],
                device_id=(q, j), device_id_type=MESH,
            ).start()
            return carry
        lax.fori_loop(1, ND, send, 0)
        pending.append((n, dst.at[pl.ds(0, ND - 1)]))

    def arrived(n, dst, peers, group=0):
        part = dst.at[pl.ds(0, peers - 1)]
        pltpu.make_async_copy(part, part, recv_sem.at[n, group]).wait()

    y = j // 4
    t0 = lax.rem(j, 4)
    xl = i // 4
    z0 = lax.rem(i, 4)

    def term_block_send(n, slot, block, dy, looped=False):
        yb = lax.rem(y + dy, 4)
        tsend[slot, pl.ds(4 * yb, 4)] = block.reshape(4, TX, LANES)
        if dy == 0:
            trecv[slot, j] = tsend[slot, j]
            pending.append((n, trecv.at[slot, pl.ds(0, NT - 1)]))

        def send(t, carry=0):
            q = 4 * yb + lax.rem(t0 + t, 4)
            pltpu.make_async_remote_copy(
                src_ref=tsend.at[slot, q], dst_ref=trecv.at[slot, j],
                send_sem=send_sem.at[n], recv_sem=recv_sem.at[n, 1 if dy == 2 else 0],
                device_id=(i, q), device_id_type=MESH,
            ).start()
            return carry

        if looped:
            lax.fori_loop(1, 4 if dy == 0 else 5, send, 0)
        else:
            for t in (2, 3, 1) if dy == 0 else (2, 3, 1, 0):
                send(t)

    def doc_block_send(n, slot, block, dx, looped=False):
        xb = lax.rem(xl + dx, 2)
        dsend[slot, pl.ds(4 * xb, 4)] = block.reshape(4, DX, LANES)
        if dx == 0:
            drecv[slot, i] = dsend[slot, i]
            pending.append((n, drecv.at[slot, pl.ds(0, ND - 1)]))

        def send(t, carry=0):
            q = 4 * xb + lax.rem(z0 + t, 4)
            pltpu.make_async_remote_copy(
                src_ref=dsend.at[slot, q], dst_ref=drecv.at[slot, i],
                send_sem=send_sem.at[n], recv_sem=recv_sem.at[n, dx],
                device_id=(q, j), device_id_type=MESH,
            ).start()
            return carry

        if looped:
            lax.fori_loop(1, 4 if dx == 0 else 5, send, 0)
        else:
            for t in (2, 1, 3) if dx == 0 else (2, 1, 3, 0):
                send(t)

    def forward_exchange(n, slot, x):
        lane_slot = iota((TILE, LANES), 1) // BLOCK
        weights = []
        for k in range(SLOTS):
            masked = [jnp.where(lane_slot == k, part, 0.0).astype(BF16) for part in x]
            weights.append(masked[0] if len(masked) == 1 else jnp.concatenate(masked, axis=1))
        for pair in ((2, 1), (3, 0)):
            rows = [pl.ds(pl.multiple_of(128 * lax.rem(y + dy, 4), 128), 128) for dy in pair]
            total = None
            for k in range(SLOTS):
                lhs = jnp.concatenate([tiles_v[k, r, :] for r in rows], axis=0)
                part = dot(lhs, weights[k], NN, None)
                total = part if total is None else total + part
            if len(x) == 2:
                total = total[:, :LANES] + total[:, LANES:]
            term_block_send(n, slot, total[:128], pair[0])
            term_block_send(n, slot, total[128:], pair[1])

    def term_sum(n, slot):
        acc = None
        for rel in (0, 1, 3, 2):
            if rel == 0:
                arrived(n, trecv.at[slot], 12)
            if rel == 2:
                arrived(n, trecv.at[slot], 5, 1)
            yb = lax.rem(y + rel, 4)
            block = trecv[slot, pl.ds(4 * yb, 4)]
            flat = jnp.concatenate([block[t] for t in range(4)], axis=1)
            onehot = st_v[:, pl.ds(pl.multiple_of(512 * yb, 512), 512)]
            part = dot(halves(flat), onehot, NTR, None)
            acc = part if acc is None else acc + part
        return acc[:TX] + acc[TX:]

    def term_gather(n, slot, x):
        both = halves(x)
        for dy in (2, 1, 3, 0):
            yb = lax.rem(y + dy, 4)
            part = dot(both, st_v[:, pl.ds(pl.multiple_of(512 * yb, 512), 512)], NN, None)
            term_block_send(n, slot, stacked(part[:TX] + part[TX:], 4), dy, dy in (0, 2))

    def doc_sum(n, slot):
        acc = None
        for dx in (0, 1):
            arrived(n, drecv.at[slot], 4 + dx, dx)
            xb = lax.rem(xl + dx, 2)
            block = drecv[slot, pl.ds(4 * xb, 4)]
            flat = jnp.concatenate([block[t] for t in range(4)], axis=1)
            onehot = sd_v[:, pl.ds(pl.multiple_of(512 * xb, 512), 512)]
            part = dot(halves(flat), onehot, NTR, None)
            acc = part if acc is None else acc + part
        return acc[:DX] + acc[DX:]

    def doc_gather(n, slot, x):
        both = halves(x)
        for dx in (1, 0):
            xb = lax.rem(xl + dx, 2)
            part = dot(both, sd_v[:, pl.ds(pl.multiple_of(512 * xb, 512), 512)], NN, None)
            doc_block_send(n, slot, stacked(part[:DX] + part[DX:], 4), dx, True)

    def split(x):
        hi = x.astype(BF16).astype(F32)
        return [hi, x - hi]

    def stacked(x, groups):
        return jnp.concatenate([x[:, g * LANES : (g + 1) * LANES] for g in range(groups)], axis=0)

    def flat_of(x, groups):
        n = x.shape[0] // groups
        return jnp.concatenate([x[g * n : (g + 1) * n] for g in range(groups)], axis=1)

    def pack(x, out):
        group = iota((8, LANES), 1) // (2 * BLOCK)
        for g in range(DGROUPS):
            rows = [x[g * TX + 8 * h : g * TX + 8 * (h + 1)] for h in range(4)]
            for m in range(4):
                total = None
                for h in range(4):
                    shift = (32 * (h - m)) % LANES
                    turned = rows[h] if shift == 0 else roll(rows[h], shift)
                    total = turned if total is None else jnp.where(group == h, turned, total)
                out[4 * g + m] = total

    def unpack(ref):
        rows = []
        for q in range(NT):
            for h in range(4):
                rows.append(ref[q] if h == 0 else roll(ref[q], LANES - 32 * h))
        return jnp.concatenate(rows, axis=0)

    def all_sum(n, base, z):
        za[n, i] = z
        to_docs(base, lambda q: za.at[n, i], za.at[n])

        def rest():
            arrived(base, za.at[n], ND)
            s = za[n, 0]
            for q in range(1, ND):
                s = s + za[n, q]
            zb[n, j] = s
            to_terms(base + 1, lambda q: zb.at[n, j], zb.at[n])

        def last():
            arrived(base + 1, zb.at[n], NT)
            s = zb[n, 0]
            for q in range(1, NT):
                s = s + zb[n, q]
            return s

        return rest, last

    pltpu.make_async_copy(start_v, start_v, load_sem.at[SLOTS]).wait()
    acc = jnp.zeros((2 * LANES, 2 * LANES), F32)
    for ch in range(8):
        both = halves(start_v[ch * 8 : (ch + 1) * 8].reshape(LANES, TILE))
        acc = acc + dot(both, both, NTR, None)
    t = acc[:LANES, :LANES] + acc[:LANES, LANES:] + acc[LANES:, :LANES] + acc[LANES:, LANES:]
    start_gram = packed(fold(t) * (1.0 / N_TERMS), None)

    cnt_load.wait()
    rows_load.wait()
    cols_load.wait()
    lane8 = iota((8, LANES), 1)
    sub8 = iota((8, LANES), 0)
    cnt = cnt_s[0, 0]
    row_at = jnp.zeros((8, LANES), jnp.int32)
    my_col = jnp.zeros((8, LANES), jnp.int32)
    col_of = jnp.zeros((8, LANES), jnp.int32)
    row_of = jnp.zeros((8, LANES), jnp.int32)
    for k in range(SLOTS):
        here = lane8 // BLOCK == k
        row_at = jnp.where(here, rows_s[0, k] * BLOCK, row_at)
        my_col = jnp.where(here, cols_s[0, k], my_col)
        col_of = jnp.where(sub8 == k, cols_s[0, k], col_of)
        row_of = jnp.where(sub8 == k, rows_s[0, k], row_of)
    row_at = jnp.where(lane8 // BLOCK < cnt, row_at, -100000)
    my_col = jnp.where(lane8 // BLOCK < cnt, my_col, -10000)
    col_of = jnp.where(sub8 < cnt, col_of, -10000)
    row_of = jnp.where(sub8 < cnt, row_of, -10000)
    col_at = my_col * BLOCK
    row_at = (row_at + lane8 % BLOCK).astype(F32)
    col_at = (col_at + lane8 % BLOCK).astype(F32)
    my_col = my_col.astype(F32)
    d1_v[i] = jnp.concatenate([col_of.astype(F32), col_at], axis=0)
    m1_v[j] = jnp.concatenate([start_gram, row_at, row_of.astype(F32)], axis=0)

    col_sums = jnp.zeros((16, TILE), F32)
    for k in range(SLOTS):
        loads[k].wait()
        ones = jnp.where(iota((16, TILE), 0) == k, 1.0, 0.0).astype(BF16)
        col_sums = col_sums + dot(ones, tiles_v[k], NN, None)
    cs_v[i] = col_sums[:SLOTS]

    pl.semaphore_wait(bar, ND - 1 + NT - 1)
    to_terms(2, lambda q: m1_v.at[j], m1_v)
    to_docs(0, lambda q: d1_v.at[i], d1_v)
    to_docs(1, lambda q: cs_v.at[i], cs_v)

    row_sums = jnp.zeros((16, TILE), F32)
    for k in range(SLOTS):
        ones = jnp.where(iota((16, TILE), 0) == k, 1.0, 0.0).astype(BF16)
        row_sums = row_sums + dot(ones, tiles_v[k], NTR, None)
    for g in range(DGROUPS):
        rs_v[g] = row_sums[:SLOTS, g * LANES : (g + 1) * LANES]
    rsr_v[j] = rs_v[j // 4]
    to_terms(3, lambda q: rs_v.at[q // 4], rsr_v)
    slots_t = jnp.concatenate([start_v[cols_s[0, k]] for k in range(SLOTS)], axis=0).T
    slots_v[...] = slots_t

    arrived(0, d1_v, ND)
    arrived(1, cs_v, ND)
    arrived(2, m1_v, NT)
    cols_in = jnp.concatenate([d1_v[q, 0:8, :] for q in range(ND)], axis=0)
    sums_t = jnp.concatenate([cs_v[q] for q in range(ND)], axis=0).T
    cst_v[...] = sums_t
    same_col = jnp.where(cols_in == my_col[0:1, :], 1.0, 0.0)
    col_scale = lax.rsqrt(dot(sums_t, same_col, NN) + 1.0)
    scaled_slots = slots_v[...] * col_scale
    gram = m1_v[0, 0:8, :]
    for q in range(1, NT):
        gram = gram + m1_v[q, 0:8, :]
    _, inverse0 = factor(unpacked(gram, 0))
    k0 = spread(inverse0)
    forward_exchange(4, 1, [dot(scaled_slots, k0, NTR)])

    for q in range(NT):
        hit = iota((DOC_TILES * BLOCK, LANES), 0).astype(F32) == m1_v[q, 8:9, :]
        st_v[:, q * LANES : (q + 1) * LANES] = jnp.where(hit, 1.0, 0.0).astype(BF16)
    rows_in = jnp.concatenate([m1_v[q, 16:24, :] for q in range(NT)], axis=0)
    rows_wide = jnp.concatenate([rows_in] * DGROUPS, axis=1)
    row_tile = (iota((LANES, DOC_TILES * BLOCK), 1) // BLOCK).astype(F32)
    same_row = jnp.where(rows_wide == row_tile, 1.0, 0.0)
    arrived(3, rsr_v, NT)
    rst_v[...] = jnp.concatenate([rsr_v[q] for q in range(NT)], axis=0).T
    my_rows = rst_v[pl.ds(pl.multiple_of(TX * lax.rem(j, 4), TX), TX), :]
    row_scale = lax.rsqrt(dot(my_rows, same_row, NN) + 1.0)
    row_square = row_scale * row_scale

    image = term_sum(4, 1)
    term_gather(5, 2, image * row_square)
    f0 = stacked(image * row_scale, DGROUPS)
    rest, last = all_sum(0, 6, packed(fold(dot(f0, f0, TN)) * (1.0 / N_DOCS), None))
    pack(f0, pk_v.at[0])
    pkr_v[0, j] = pk_v[0, j]
    to_terms(8, lambda q: pk_v.at[0, q], pkr_v.at[0])

    for q in range(ND):
        hit = iota((TERM_TILES * BLOCK, LANES), 0).astype(F32) == d1_v[q, 8:9, :]
        sd_v[:, q * LANES : (q + 1) * LANES] = jnp.where(hit, 1.0, 0.0).astype(BF16)
    rest()
    arrived(5, trecv.at[2], 12)
    arrived(5, trecv.at[2], 5, 1)
    pieces = jnp.concatenate([trecv[2, q] for q in range(NT)], axis=0).T
    hi = pieces.astype(BF16)
    lo = (pieces - hi.astype(F32)).astype(BF16)
    pairs = []
    for k in range(SLOTS):
        part = slice(k * BLOCK, (k + 1) * BLOCK)
        pairs.append(jnp.concatenate([hi[part], lo[part]], axis=0))
    for dx in (1, 0):
        columns = pl.ds(pl.multiple_of(256 * lax.rem(xl + dx, 2), 256), 256)
        back = []
        for k in range(SLOTS):
            both = dot(pairs[k], tiles_v[k, :, columns], NN, None)
            back.append(both[:BLOCK] + both[BLOCK:])
        doc_block_send(9, 0, jnp.concatenate(back, axis=0).T, dx)

    cols_wide = jnp.concatenate([cols_in] * TGROUPS, axis=1)
    tile_at = (iota((ND * SLOTS, TERM_TILES * BLOCK), 1) // BLOCK).astype(F32)
    my_sums = cst_v[pl.ds(pl.multiple_of(i * DX, DX), DX), :]
    col_share = lax.rsqrt(dot(my_sums, jnp.where(cols_wide == tile_at, 1.0, 0.0), NN) + 1.0)
    col_square = col_share * col_share
    window = pl.ds(pl.multiple_of(128 * (i // 2), 128), 128)
    for g in range(TGROUPS):
        share_v[g] = start_v[g * 8 : (g + 1) * 8, :, window].reshape(LANES, 128).T
    half = pl.multiple_of(DX * lax.rem(i, 2), DX)
    start_share = jnp.concatenate([share_v[g, pl.ds(half, DX), :] for g in range(TGROUPS)], axis=0)
    e_share = dot(start_share, k0, NTR)
    upper1, inverse1 = factor(unpacked(last(), 0))
    k1 = spread(inverse1)
    p0 = upper1 * (N_DOCS / N_TERMS)
    expected = dot(e_share, spread(p0), NTR)
    u1 = dot(f0, k1, NTR)

    image = doc_sum(9, 0)
    doc_gather(10, 1, image * col_square)
    b1 = dot(stacked(image * col_share, TGROUPS), k1, NTR) - expected
    t2 = dot(b1, jnp.concatenate([b1, e_share], axis=1), TN) * (1.0 / N_TERMS)
    rest, last = all_sum(1, 11, packed(fold(t2[:, :LANES]), fold(t2[:, LANES:])))
    for g in range(TGROUPS):
        share_v[g, 0:DX, :] = b1[g * DX : (g + 1) * DX]
    drecv[2, i] = share_v[i, 0:DX, :]

    rest()
    arrived(10, drecv.at[1], 4)
    arrived(10, drecv.at[1], 5, 1)
    pieces = jnp.concatenate([drecv[1, q] for q in range(ND)], axis=0)
    forward_exchange(14, 3, split(pieces))
    to_docs(13, lambda q: share_v.at[q, pl.ds(0, DX), :], drecv.at[2])
    z = last()
    r1 = unpacked(z, 2)
    pad = jnp.zeros((LANES - BLOCK, LANES), F32)
    g2 = unpacked(z, 0) - dot(r1, jnp.concatenate([r1, pad], axis=0), NTR)
    upper2, inverse2 = factor(g2)
    k2 = spread(inverse2)
    kr1 = spread(r1)
    p02 = upper2 * (N_TERMS / N_DOCS)
    k21 = dot(k2, k1, NN)
    known = dot(k2, spread(p0 + r1), NN) + dot(spread(p02), k1, NN)
    expected = dot(f0, known, NTR)

    image = term_sum(14, 3) * row_scale
    x2 = dot(stacked(image, DGROUPS), k21, NTR) - expected
    t3 = dot(x2, jnp.concatenate([x2, u1], axis=1), TN) * (1.0 / N_DOCS)
    rest, last = all_sum(2, 15, packed(fold(t3[:, :LANES]), fold(t3[:, LANES:])))
    pack(x2, pk_v.at[1])
    pkr_v[1, j] = pk_v[1, j]
    to_terms(17, lambda q: pk_v.at[1, q], pkr_v.at[1])
    rest()
    arrived(13, drecv.at[2], ND)
    right_x = jnp.concatenate([drecv[2, q] for q in range(ND)], axis=0)

    start_st = start_v[pl.ds(i * 8, 8)].reshape(LANES, TILE)
    k20 = dot(k2, dot(kr1, k0, NN), NN)
    right = dot(k2, right_x, NTR) - dot(k20, start_st, NN)
    for g in range(8):
        right_o[:, g * TILE : (g + 1) * TILE] = right[g * BLOCK : (g + 1) * BLOCK]
    coef_o[0] = transposed(upper1)[:, :BLOCK]
    coef_o[1] = (p0 + r1)[:, :BLOCK]
    coef_o[2] = transposed(upper2)[:, :BLOCK]
    arrived(8, pkr_v.at[0], NT)
    left_u = dot(unpack(pkr_v.at[0]), k1, NTR)
    arrived(17, pkr_v.at[1], NT)
    left_x = unpack(pkr_v.at[1])

    z = last()
    r2 = unpacked(z, 2)
    g3 = unpacked(z, 0) - dot(r2, jnp.concatenate([r2, pad], axis=0), NTR)
    upper3, inverse3 = factor(g3)
    left_x = left_x - dot(left_u, spread(r2), NTR)
    rep = inverse3 + roll(inverse3, 16)
    rep = rep + roll(rep, 32)
    rep = rep + roll(rep, 64)
    mine = iota((2 * BLOCK, LANES), 1) // BLOCK == iota((2 * BLOCK, LANES), 0) // BLOCK
    left = dot(jnp.where(mine, jnp.concatenate([rep, rep], axis=0), 0.0), left_x, NTR)
    left_o[:, 0:TILE] = left[0:BLOCK]
    left_o[:, TILE : 2 * TILE] = left[BLOCK : 2 * BLOCK]
    coef_o[3] = (p02 + r2)[:, :BLOCK]
    coef_o[4] = transposed(upper3)[:, :BLOCK]
    for n, part in pending:
        pltpu.make_async_copy(part, part, send_sem.at[n]).wait()


def hand_over(left_i, right_i, coef_i, left_o, right_o, coef_o):
    left_o[...] = left_i[...]
    right_o[...] = right_i[...]
    coef_o[...] = coef_i[...]


def on_device(tiles, tile_rows, tile_cols, counts, start_block):
    anywhere = pl.BlockSpec(memory_space=pl.ANY)
    vmem = pl.BlockSpec(memory_space=pltpu.VMEM)
    shapes = (
        jax.ShapeDtypeStruct((BLOCK, DOC_TILES * TILE // NT), F32),
        jax.ShapeDtypeStruct((BLOCK, TERM_TILES * TILE // ND), F32),
        jax.ShapeDtypeStruct((5, BLOCK, BLOCK), F32),
    )
    results = pl.pallas_call(
        kernel,
        out_shape=shapes,
        in_specs=[anywhere] * 5,
        out_specs=(vmem, vmem, vmem),
        scratch_shapes=[
            pltpu.SMEM((1, 1), jnp.int32),
            pltpu.SMEM((1, SLOTS), jnp.int32),
            pltpu.SMEM((1, SLOTS), jnp.int32),
            pltpu.VMEM((SLOTS, TILE, TILE), BF16),
            pltpu.VMEM((TERM_TILES, BLOCK, TILE), F32),
            pltpu.VMEM((DOC_TILES * BLOCK, NT * LANES), BF16),
            pltpu.VMEM((TERM_TILES * BLOCK, ND * LANES), BF16),
            pltpu.VMEM((NT, 24, LANES), F32),
            pltpu.VMEM((ND, 16, LANES), F32),
            pltpu.VMEM((ND, SLOTS, TILE), F32),
            pltpu.VMEM((4, NT, TX, LANES), F32),
            pltpu.VMEM((4, NT, TX, LANES), F32),
            pltpu.VMEM((2, ND, DX, LANES), F32),
            pltpu.VMEM((3, ND, DX, LANES), F32),
            pltpu.VMEM((3, ND, 8, LANES), F32),
            pltpu.VMEM((3, NT, 8, LANES), F32),
            pltpu.VMEM((TILE, LANES), F32),
            pltpu.VMEM((TGROUPS, LANES, LANES), F32),
            pltpu.VMEM((TILE, ND * SLOTS), F32),
            pltpu.VMEM((DGROUPS, SLOTS, LANES), F32),
            pltpu.VMEM((NT, SLOTS, LANES), F32),
            pltpu.VMEM((LANES, LANES), F32),
            pltpu.VMEM((2, NT, 8, LANES), F32),
            pltpu.VMEM((2, NT, 8, LANES), F32),
            pltpu.SemaphoreType.DMA((SLOTS + 4,)),
            pltpu.SemaphoreType.DMA((18,)),
            pltpu.SemaphoreType.DMA((18, 2)),
        ],
        compiler_params=pltpu.CompilerParams(
            collective_id=0, has_side_effects=True, vmem_limit_bytes=56000000
        ),
    )(
        counts,
        tile_rows.reshape(1, SLOTS),
        tile_cols.reshape(1, SLOTS),
        tiles.reshape(SLOTS, TILE, TILE),
        start_block,
    )
    return pl.pallas_call(
        hand_over,
        out_shape=shapes,
        in_specs=[vmem, vmem, vmem],
        out_specs=(vmem, vmem, vmem),
        compiler_params=pltpu.CompilerParams(vmem_limit_bytes=8 * 1024 * 1024),
    )(*results)


def solution(mesh):
    return jax.shard_map(
        on_device,
        mesh=mesh,
        in_specs=(
            P("doc", "term", None, None, None),
            P("doc", "term", None),
            P("doc", "term", None),
            P("doc", "term"),
            P(None, "term"),
        ),
        out_specs=(P(None, ("doc", "term")), P(None, ("term", "doc")), P()),
        check_vma=False,
    )
```
